128 devices in a mesh: orb: 16 (over x_hi, z, core), grp: 8 (over x_lo, y).
Axes of the slice: x: 4 (x_hi: 2, x_lo: 2; x = x_hi * 2 + x_lo), y: 4, z: 4, core: 2. Of those that a mesh axis runs over, the one named last changes fastest.
Arguments:
- orbitals: float32 [1024, 64, 4096], P(('orb', 'grp')), may hold values from -5 to 5
- occupations: float32 [1024], P(('orb', 'grp')), may hold values from 0.5 to 2
- external: float32 [64, 4096], P('orb'), may hold values from -1.5 to 0.5
Outputs:
- applied: float32 [1024, 64, 4096], P(('orb', 'grp'))
The draws below stay inside these ranges and needn't reach their ends.
All inputs are finite; a program needn't handle non-finite values.
Results may differ from the reference program's by a relative error of at most 0.0001.
Values sent between devices are 32-bit elements; how exact they have to be, the bound alone decides.
No kernel may reach another device: no remote copies, remote signals or barrier semaphores. Data moves between devices by JAX's collectives and lax.ppermute only.
A program may use at most 256 MiB of HBM per device.

```python
import math
import jax
import jax.numpy as jnp
from jax import lax

GRID = 64
ORBS = 1024


def draw_orbitals(key, part):
    count = GRID
    coords = jnp.arange(count, dtype=jnp.float32)
    half = jnp.float32(count // 2)
    width = count / 8.0

    def one_orbital(index):
        block_key = jax.random.fold_in(jax.random.fold_in(key, 101), index // 8)
        own_key = jax.random.fold_in(jax.random.fold_in(key, 202), index)
        centre = jax.random.randint(block_key, (3,), 0, count).astype(jnp.float32)
        wave_key, phase_key, noise_key = jax.random.split(own_key, 3)
        waves = jax.random.randint(wave_key, (3, 3), -2, 3).astype(jnp.float32)
        phases = jax.random.uniform(phase_key, (3,), jnp.float32, -math.pi, math.pi)
        bumps = []
        for axis_id in range(3):
            offset = jnp.mod(coords - centre[axis_id] + half, jnp.float32(count)) - half
            bumps.append(jnp.exp(-offset * offset / jnp.float32(2.0 * width * width)))
        envelope = bumps[0][:, None, None] * bumps[1][None, :, None] * bumps[2][None, None, :]
        smooth = jnp.zeros((count, count, count), jnp.float32)
        step = jnp.float32(2.0 * math.pi / count)
        for mode in range(3):
            angle = step * (waves[mode, 0] * coords[:, None, None] + waves[mode, 1] * coords[None, :, None] + waves[mode, 2] * coords[None, None, :]) + phases[mode]
            smooth = smooth + jnp.cos(angle)
        smooth = smooth / jnp.float32(math.sqrt(1.5))
        rough = 0.15 * jnp.clip(jax.random.normal(noise_key, (count, count, count), jnp.float32), -4.0, 4.0)
        amplitude = jnp.float32(1.0)
        orbital = amplitude * envelope * (smooth + rough)
        return orbital.reshape(count, count * count).astype(jnp.float32)
    return lax.map(one_orbital, jnp.arange(ORBS, dtype=jnp.int32))


def block_levels(stream_key, shape, pieces, low, high):
    gain, own = 1.0, jax.random.fold_in(stream_key, 6)
    for axis_at, blocks in pieces:
        heights = jnp.exp(jax.random.uniform(jax.random.fold_in(own, axis_at), (blocks,), jnp.float32, low / len(pieces), high / len(pieces)))
        gain = gain * jnp.repeat(heights, shape[axis_at] // blocks).reshape([-1 if axis == axis_at else 1 for axis in range(len(shape))])
    return gain


def setup_inputs(seed: int = 0) -> dict:
    seeds = jax.random.split(jax.random.key(seed), 4)
    orbitals = draw_orbitals(jax.random.fold_in(seeds[3], 71), 0)
    occupations = jnp.clip(0.5 + 1.5 * jax.random.uniform(seeds[1], (ORBS,), jnp.float32) ** block_levels(seeds[1], (ORBS,), ((0, 128),), -0.2, 0.2), 0.5, 2.0)
    external = jnp.clip(-1.5 + 2.0 * jax.random.uniform(seeds[2], (GRID, GRID * GRID), jnp.float32) ** block_levels(seeds[2], (GRID, GRID * GRID), ((0, 16),), -0.2, 0.2), -1.5, 0.5)
    return dict(orbitals=orbitals, occupations=occupations, external=external)


MAGIC_TAPS = [8.4334247333529341094733325815816e-7, -0.1290557201342060969516786758559028e-4, 0.8762984476210559564689161894116397e-4, -0.30158038132690463167163703826169879e-3, 0.174723713672993903449447812749852942e-2, -0.942047030201080385922711540948195075e-2, 0.2373821463724942397566389712597274535e-1, 0.612625895831207982195380597e-1, 0.9940415697834003993178616713, -0.604895289196983516002834636e-1, -0.2103025160930381434955489412839065067e-1, 0.1337263414854794752733423467013220997e-1, -0.344128144493493857280881509686821861e-2, 0.49443227688689919192282259476750972e-3, -0.5185986881173432922848639136911487e-4, 2.72734492911979659657715313017228e-6]
KINETIC_HALF = [-3.5536922899131901941296809374, 2.2191465938911163898794546405, -0.6156141465570069496314853949, 0.2371780582153805636239247476, -0.0822663999742123340987663521, 0.02207029188482255523789911295638968409, -0.409765689342633823899327051188315485e-2, 0.45167920287502235349480037639758496e-3, -0.2398228524507599670405555359023135e-4, 2.0904234952920365957922889447361e-6, -3.7230763047369275848791496973044e-7, -1.05857055496741470373494132287e-8, -5.813879830282540547959250667e-11, 2.70800493626319438269856689037647576e-13, -6.924474940639200152025730585882e-18]
KINETIC_TAPS = KINETIC_HALF[:0:-1] + KINETIC_HALF
SPACING = 0.45
HIGH = lax.Precision.HIGHEST


def circulant(taps, offset, count):
    row_ids = lax.broadcasted_iota(jnp.int32, (count, count), 0)
    col_ids = lax.broadcasted_iota(jnp.int32, (count, count), 1)
    matrix = jnp.zeros((count, count), jnp.float32)
    for position, weight in enumerate(taps):
        hit = jnp.mod(col_ids - row_ids - (position - offset), count) == 0
        matrix = matrix + jnp.where(hit, jnp.float32(weight), jnp.float32(0.0))
    return matrix


def kinetic_matrix(count):
    return circulant(KINETIC_TAPS, 14, count) * jnp.float32(-0.5 / (SPACING * SPACING))


def filter_forward(field, matrix):
    field = jnp.einsum('oxyj,zj->oxyz', field, matrix, precision=HIGH)
    field = jnp.einsum('oxjz,yj->oxyz', field, matrix, precision=HIGH)
    return jnp.einsum('ojyz,xj->oxyz', field, matrix, precision=HIGH)


def filter_back(field, matrix):
    field = jnp.einsum('oxyj,jz->oxyz', field, matrix, precision=HIGH)
    field = jnp.einsum('oxjz,jy->oxyz', field, matrix, precision=HIGH)
    return jnp.einsum('ojyz,jx->oxyz', field, matrix, precision=HIGH)


def kinetic(field, matrix):
    result = jnp.einsum('oxyj,zj->oxyz', field, matrix, precision=HIGH)
    result = result + jnp.einsum('oxjz,yj->oxyz', field, matrix, precision=HIGH)
    return result + jnp.einsum('ojyz,xj->oxyz', field, matrix, precision=HIGH)


def reference(orbitals, occupations, external):
    count = orbitals.shape[1]
    magic = circulant(MAGIC_TAPS, 8, count)
    kin_matrix = kinetic_matrix(count)
    external_cube = external.reshape(count, count, count)

    def add_density(total, item):
        orbital, weight = item
        values = filter_forward(orbital.reshape(1, count, count, count), magic)[0]
        return total + weight * values * values, None

    density, _ = lax.scan(add_density, jnp.zeros((count, count, count), jnp.float32), (orbitals, occupations))
    potential = external_cube - jnp.cbrt((3.0 / math.pi) * density)

    def apply_one(orbital):
        field = orbital.reshape(1, count, count, count)
        values = filter_forward(field, magic)
        result = (filter_back(potential[None] * values, magic) + kinetic(field, kin_matrix))[0]
        return result.reshape(count, count * count)

    return lax.map(apply_one, orbitals)
```

```python
import functools
import math

import jax
import jax.numpy as jnp
import ml_dtypes
import numpy as np
from jax import lax
from jax.experimental import pallas as pl
from jax.experimental.pallas import tpu as pltpu
from jax.sharding import Mesh, PartitionSpec as P

MAGIC_TAPS = [
    8.433424733352934e-07,
    -1.290557201342061e-05,
    8.76298447621056e-05,
    -0.00030158038132690465,
    0.001747237136729939,
    -0.009420470302010804,
    0.023738214637249424,
    0.0612625895831208,
    0.9940415697834003,
    -0.06048952891969835,
    -0.021030251609303816,
    0.013372634148547948,
    -0.0034412814449349387,
    0.0004944322768868992,
    -5.185986881173433e-05,
    2.7273449291197967e-06,
]
KINETIC_HALF = [
    -3.55369228991319,
    2.2191465938911166,
    -0.615614146557007,
    0.23717805821538057,
    -0.08226639997421234,
    0.022070291884822554,
    -0.004097656893426338,
    0.00045167920287502236,
    -2.3982285245075998e-05,
    2.0904234952920368e-06,
    -3.7230763047369276e-07,
    -1.0585705549674146e-08,
    -5.8138798302825403e-11,
    2.7080049362631943e-13,
    -6.9244749406392e-18,
]
KINETIC_TAPS = KINETIC_HALF[:0:-1] + KINETIC_HALF
SPACING = 0.45

N = 64
GROUP = 4
ROWS = GROUP * N
BF16 = ml_dtypes.bfloat16
AXES = ("xh", "z", "core", "xl", "y")
CHIPS = ("xh", "z", "xl", "y")
PARAMS = dict(vmem_limit_bytes=60 * 2**20)


def circulant(taps, offset):
    matrix = np.zeros((N, N), np.float32)
    for position, weight in enumerate(taps):
        for row in range(N):
            matrix[row, (row + position - offset) % N] += np.float32(weight)
    return matrix


def halves(matrix):
    high = matrix.astype(BF16)
    return high, (matrix - high.astype(np.float32)).astype(BF16)


def lane_operator(matrix):
    high, low = halves(np.kron(np.eye(2, dtype=np.float32), matrix))
    return np.concatenate([np.concatenate([high, high], 1), np.concatenate([low, np.zeros_like(low)], 1)])


def band_operator(taps):
    band = np.zeros((16, 32), np.float32)
    for out in range(16):
        for position, weight in enumerate(taps):
            band[out, out + position] = np.float32(weight)
    high, low = halves(np.kron(band, np.eye(8, dtype=np.float32)))
    return np.concatenate([high, low])


MAGIC = circulant(MAGIC_TAPS, 8)
KINETIC = circulant(KINETIC_TAPS, 14) * np.float32(-0.5 / (SPACING * SPACING))
LANE_M = lane_operator(MAGIC)
LANE_MT = lane_operator(MAGIC.T)
BAND_M = band_operator(MAGIC_TAPS)
BAND_MT = band_operator(MAGIC_TAPS[::-1])
LANE_K = lane_operator(KINETIC)
LANE_ONE = np.concatenate([np.eye(128), np.eye(128)], 1).astype(BF16)
LANE_ONE_K = np.concatenate([LANE_ONE, LANE_K])
ROW_K = np.concatenate(halves(np.kron(KINETIC, np.eye(8, dtype=np.float32))))


def split(block):
    high = block.astype(jnp.bfloat16)
    return high, (block - high.astype(jnp.float32)).astype(jnp.bfloat16)


def turned(operator, block):
    both = jnp.concatenate(split(block), axis=1)
    return lax.dot_general(operator, both, (((1,), (1,)), ((), ())), preferred_element_type=jnp.float32)


def dot(left, right):
    return lax.dot_general(left, right, (((1,), (0,)), ((), ())), preferred_element_type=jnp.float32)


def store_padded(ref, y, block, before, after):
    ref[pl.ds(y + before, 2)] = block

    @pl.when(y >= N - before)
    def _():
        ref[pl.ds(jnp.maximum(y + before - N, 0), 2)] = block

    @pl.when(y < after)
    def _():
        ref[pl.ds(y + before + N, 2)] = block


def band_rows(source, target, operator, shift):
    def step(index, _):
        z = pl.multiple_of(index * 8, 8)
        for start in range(0, N, 16):
            window = source[pl.ds(start + shift, 32), pl.ds(z, 8), :].reshape(256, ROWS)
            high, low = split(window)
            main = dot(operator, high)
            rest = dot(operator[:128], low)
            result = main[:128] + main[128:] + rest
            target[pl.ds(start, 16), pl.ds(z, 8), :] = result.reshape(16, 8, ROWS)
        return 0

    lax.fori_loop(0, N // 8, step, 0)


def forward_kernel(core_ref, occ_ref, lane_ref, band_ref, orb_ref, val_ref, keep_ref, send_ref, first, second, total, spread):
    group = pl.program_id(0)
    lane_op, band_op = lane_ref[...], band_ref[...]

    def along_z(index, _):
        for part in range(2):
            tile = index * 2 + part
            lanes = pl.ds(pl.multiple_of(tile * 128, 128), 128)
            block = orb_ref[:, :, lanes].reshape(ROWS, 128)
            out = turned(lane_op, block)
            store_padded(first, tile * 2, (out[:128] + out[128:]).reshape(2, N, ROWS), 8, 10)
        return 0

    lax.fori_loop(0, 16, along_z, 0)
    band_rows(first, second, band_op, 0)

    def along_x(index, _):
        lanes = pl.ds(pl.multiple_of(index * 256, 256), 256)
        density = jnp.zeros((N, 256), jnp.float32)
        for pair in range(2):
            block = second[pl.ds(index * 4, 4), :, pair * 128 : pair * 128 + 128].reshape(256, 128)
            out = turned(lane_op, block)
            out = (out[:128] + out[128:]).reshape(2, N, 256)
            val_ref[pair * 2 : pair * 2 + 2, :, lanes] = out
            for one in range(2):
                density = density + occ_ref[group * GROUP + pair * 2 + one] * (out[one] * out[one])
        before = jnp.where(group == 0, jnp.zeros_like(density), total[:, lanes])
        total[:, lanes] = before + density
        return 0

    lax.fori_loop(0, 16, along_x, 0)

    @pl.when(group == pl.num_programs(0) - 1)
    def _():
        for tile in range(32):
            spread[:, tile, :] = total[:, tile * 128 : tile * 128 + 128]
        core = core_ref[0]
        for block in range(8):
            keep_ref[block] = spread[pl.ds(block * 8 + core * 4, 4)]
            send_ref[block] = spread[pl.ds(block * 8 + 4 - core * 4, 4)]


def back_kernel(core_ref, lane_ref, band_ref, own_ref, other_ref, val_ref, kin0_ref, kin1_ref, out_ref, first, second, total, spread):
    group = pl.program_id(0)
    lane_op, band_op = lane_ref[...], band_ref[...]

    @pl.when(group == 0)
    def _():
        core = core_ref[0]
        for block in range(8):
            spread[pl.ds(block * 8 + core * 4, 4)] = own_ref[block]
            spread[pl.ds(block * 8 + 4 - core * 4, 4)] = other_ref[block]
        for tile in range(32):
            total[:, tile * 128 : tile * 128 + 128] = spread[:, tile, :]

    def along_z(index, _):
        for part in range(2):
            tile = index * 2 + part
            lanes = pl.ds(pl.multiple_of(tile * 128, 128), 128)
            block = (val_ref[:, :, lanes] * total[:, lanes][None]).reshape(ROWS, 128)
            out = turned(lane_op, block)
            store_padded(first, tile * 2, (out[:128] + out[128:]).reshape(2, N, ROWS), 8, 10)
        return 0

    lax.fori_loop(0, 16, along_z, 0)
    band_rows(first, second, band_op, 1)

    def along_x(kin_ref, index, _):
        lanes = pl.ds(pl.multiple_of(index * 256, 256), 256)
        for pair in range(2):
            block = second[pl.ds(index * 4, 4), :, pair * 128 : pair * 128 + 128].reshape(256, 128)
            out = turned(lane_op, block)
            two = slice(pair * 2, pair * 2 + 2)
            out_ref[two, :, lanes] = (out[:128] + out[128:]).reshape(2, N, 256) + kin_ref[two, :, lanes]
        return 0

    for which, kin_ref in enumerate((kin0_ref, kin1_ref)):

        @pl.when(group == which)
        def _():
            lax.fori_loop(0, 16, functools.partial(along_x, kin_ref), 0)


def kinetic_kernel(_, one_ref, lane_ref, row_ref, orb_ref, out_ref, first, second):
    one_op, lane_op = one_ref[...], lane_ref[...]

    def along_z(index, _):
        for part in range(2):
            tile = index * 2 + part
            lanes = pl.ds(pl.multiple_of(tile * 128, 128), 128)
            out = turned(one_op, orb_ref[:, :, lanes].reshape(ROWS, 128))
            first[pl.ds(tile * 2, 2)] = out[:128].reshape(2, N, ROWS)
            second[pl.ds(tile * 2, 2)] = (out[128:256] + out[256:]).reshape(2, N, ROWS)
        return 0

    lax.fori_loop(0, 16, along_z, 0)

    def along_y(index, _):
        rows = pl.ds(pl.multiple_of(index * 8, 8), 8)
        high, low = split(first[:, rows, :].reshape(512, ROWS))
        out = dot(row_ref[:512], high) + dot(row_ref[512:], high) + dot(row_ref[:512], low)
        second[:, rows, :] = second[:, rows, :] + out.reshape(N, 8, ROWS)
        return 0

    lax.fori_loop(0, 8, along_y, 0)

    def along_x(index, _):
        lanes = pl.ds(pl.multiple_of(index * 256, 256), 256)
        for pair in range(2):
            block = (pl.ds(index * 4, 4), slice(None), slice(pair * 128, pair * 128 + 128))
            rest = turned(one_op[:128], second[block].reshape(256, 128))
            out = turned(lane_op, first[block].reshape(256, 128))
            out_ref[pair * 2 : pair * 2 + 2, :, lanes] = (out[:128] + out[128:] + rest).reshape(2, N, 256)
        return 0

    lax.fori_loop(0, 16, along_x, 0)


SMEM = pl.BlockSpec(memory_space=pltpu.SMEM)
ORBITALS = pl.BlockSpec((GROUP, N, N * N), lambda group: (group, 0, 0))
PADDED = pltpu.VMEM((N + 18, N, ROWS), jnp.float32)
PLAIN = pltpu.VMEM((N, N, ROWS), jnp.float32)
PLANES = pltpu.VMEM((N, N * N), jnp.float32)
SPREAD = pltpu.VMEM((N, 32, 128), jnp.float32)
HALF = jax.ShapeDtypeStruct((8, 4, 32, 128), jnp.float32)


def whole(shape):
    return pl.BlockSpec(shape, lambda *_: (0,) * len(shape), pipeline_mode=pl.Buffered(1))


def cost(rows, bytes_accessed):
    return pl.CostEstimate(flops=rows * 2 * 256 * 256, bytes_accessed=bytes_accessed, transcendentals=0)


def forward(core, occupations, orbitals):
    count = orbitals.shape[0]
    return pl.pallas_call(
        forward_kernel,
        grid=(count // GROUP,),
        in_specs=[SMEM, SMEM, whole((256, 256)), whole((256, 256)), ORBITALS],
        out_specs=[ORBITALS, whole(HALF.shape), whole(HALF.shape)],
        out_shape=[jax.ShapeDtypeStruct(orbitals.shape, jnp.float32), HALF, HALF],
        scratch_shapes=[PADDED, PLAIN, PLANES, SPREAD],
        compiler_params=pltpu.CompilerParams(**PARAMS),
        cost_estimate=cost(57344, 18 * 2**20),
        name="forward",
    )(core, occupations, jnp.asarray(LANE_M), jnp.asarray(BAND_M), orbitals)


def back(core, own, other, values, kin0, kin1):
    count = values.shape[0]
    return pl.pallas_call(
        back_kernel,
        grid=(count // GROUP,),
        in_specs=[SMEM, whole((256, 256)), whole((256, 256)), whole(HALF.shape), whole(HALF.shape), ORBITALS, whole((GROUP, N, N * N)), whole((GROUP, N, N * N))],
        out_specs=ORBITALS,
        out_shape=jax.ShapeDtypeStruct(values.shape, jnp.float32),
        scratch_shapes=[PADDED, PLAIN, PLANES, SPREAD],
        compiler_params=pltpu.CompilerParams(**PARAMS),
        cost_estimate=cost(57344, 26 * 2**20),
        name="back",
    )(core, jnp.asarray(LANE_MT), jnp.asarray(BAND_MT), own, other, values, kin0, kin1)


def kinetic(after, orbitals, group):
    block = (GROUP, N, N * N)
    return pl.pallas_call(
        kinetic_kernel,
        grid=(1,),
        in_specs=[SMEM, whole((384, 256)), whole((256, 256)), whole((1024, 512)), pl.BlockSpec(block, lambda _: (group, 0, 0))],
        out_specs=pl.BlockSpec(block, lambda _: (0, 0, 0)),
        out_shape=jax.ShapeDtypeStruct(block, jnp.float32),
        scratch_shapes=[PLAIN, PLAIN],
        compiler_params=pltpu.CompilerParams(**PARAMS),
        cost_estimate=cost(49152, 9 * 2**20),
        name=f"kinetic{group}",
    )(after, jnp.asarray(LANE_ONE_K), jnp.asarray(LANE_K), jnp.asarray(ROW_K), orbitals)


SWAP = [(0, 1), (1, 0)]


def on_device(orbitals, occupations, external):
    core = lax.axis_index("core").astype(jnp.int32).reshape(1)
    member = lax.axis_index("xl") * 4 + lax.axis_index("y")
    own_external = lax.dynamic_index_in_dim(external.reshape(8, 16, 128), member, 0, keepdims=False)
    values, keep, send = forward(core, occupations, orbitals)
    partial = (keep + lax.ppermute(send, "core", SWAP)).reshape(64, 16, 128)
    partial, after = lax.optimization_barrier((partial, core))
    shares = lax.all_to_all(partial, CHIPS, 0, 0, tiled=True)
    shares, kin0 = lax.optimization_barrier((shares, kinetic(after, orbitals, 0)))
    density = jnp.sum(shares, axis=0)
    potential = own_external - jnp.cbrt(3.0 / math.pi * density)
    copies, after = lax.optimization_barrier((jnp.broadcast_to(potential[None], (64, 16, 128)), core))
    own = lax.all_to_all(copies, CHIPS, 0, 0, tiled=True)
    own, kin1 = lax.optimization_barrier((own, kinetic(after, orbitals, 1)))
    own = own.reshape(HALF.shape)
    other = lax.ppermute(own, "core", SWAP)
    return back(core, own, other, values, kin0, kin1)


def solution(mesh):
    fine = Mesh(mesh.devices.reshape(2, 4, 2, 2, 4), AXES)
    orb = ("xh", "z", "core")
    return jax.shard_map(
        on_device,
        mesh=fine,
        in_specs=(P(AXES, None, None), P(AXES), P(orb, None)),
        out_specs=P(AXES, None, None),
        check_vma=False,
    )
```

```python
import functools
import math

import jax
import jax.numpy as jnp
import ml_dtypes
import numpy as np
from jax import lax
from jax.experimental import pallas as pl
from jax.experimental.pallas import tpu as pltpu
from jax.sharding import Mesh, PartitionSpec as P

MAGIC_TAPS = [
    8.433424733352934e-07,
    -1.290557201342061e-05,
    8.76298447621056e-05,
    -0.00030158038132690465,
    0.001747237136729939,
    -0.009420470302010804,
    0.023738214637249424,
    0.0612625895831208,
    0.9940415697834003,
    -0.06048952891969835,
    -0.021030251609303816,
    0.013372634148547948,
    -0.0034412814449349387,
    0.0004944322768868992,
    -5.185986881173433e-05,
    2.7273449291197967e-06,
]
KINETIC_HALF = [
    -3.55369228991319,
    2.2191465938911166,
    -0.615614146557007,
    0.23717805821538057,
    -0.08226639997421234,
    0.022070291884822554,
    -0.004097656893426338,
    0.00045167920287502236,
    -2.3982285245075998e-05,
    2.0904234952920368e-06,
    -3.7230763047369276e-07,
    -1.0585705549674146e-08,
    -5.8138798302825403e-11,
    2.7080049362631943e-13,
    -6.9244749406392e-18,
]
KINETIC_TAPS = KINETIC_HALF[:0:-1] + KINETIC_HALF
SPACING = 0.45

N = 64
GROUP = 4
ROWS = GROUP * N
PAIRS = N // 2
BF16 = ml_dtypes.bfloat16
AXES = ("xh", "z", "core", "xl", "y")
CHIPS = ("xh", "xl", "y", "z")
PARAMS = dict(vmem_limit_bytes=60 * 2**20)
UNROLL = 16


def circulant(taps, offset):
    matrix = np.zeros((N, N), np.float32)
    for position, weight in enumerate(taps):
        for row in range(N):
            matrix[row, (row + position - offset) % N] += np.float32(weight)
    return matrix


def halves(matrix):
    high = matrix.astype(BF16)
    return high, (matrix - high.astype(np.float32)).astype(BF16)


MIXED = np.arange(128).reshape(2, 16, 4).transpose(1, 0, 2).reshape(128)


def lane_operator(matrix, order=slice(None)):
    return np.concatenate([np.concatenate([part, part], 1)[order] for part in halves(np.kron(np.eye(2, dtype=np.float32), matrix))])


def slow_operator(matrix):
    return np.concatenate(halves(np.kron(matrix, np.eye(4, dtype=np.float32))))


MAGIC = circulant(MAGIC_TAPS, 8)
KINETIC = circulant(KINETIC_TAPS, 14) * np.float32(-0.5 / (SPACING * SPACING))
CENTRE = float(np.float32(3.0) * KINETIC[0, 0])
SIDES = KINETIC - np.diag(np.diag(KINETIC))
ONE = np.eye(N, dtype=np.float32)


def split(block):
    high = block.astype(jnp.bfloat16)
    return high, (block - high.astype(jnp.float32)).astype(jnp.bfloat16)


def both(block):
    return jnp.concatenate(split(block), axis=1)


def run(jobs):
    queues = []
    for unit, queue in enumerate(jobs):
        steps = []
        for index, (parts, accs, finish) in enumerate(queue):
            for at, part in enumerate(parts):
                steps.append((part, accs, finish if at == len(parts) - 1 else None))
        queues.append(steps)
    pending = [None] * len(queues)

    def push(unit, at):
        (operand, transpose, _), _, _ = queues[unit][at]
        pltpu.matmul_push_rhs(operand(), at % 2, unit, transpose=transpose)

    for unit in range(len(queues)):
        push(unit, 0)
    for at in range(len(queues[0])):
        for unit, queue in enumerate(queues):
            if at + 1 < len(queue):
                push(unit, at + 1)
            (_, _, products), accs, finish = queue[at]
            for which, (acc, left) in enumerate(products):
                pltpu.matmul_acc_lhs(accs[acc], left(), load_staged_rhs=at % 2 if which == 0 else None)
            if pending[unit] is not None:
                done, held = pending[unit]
                done(*[pltpu.matmul_pop(acc) for acc in held])
                pending[unit] = None
            if finish is not None:
                pending[unit] = (finish, accs)
    for done, held in pending:
        done(*[pltpu.matmul_pop(acc) for acc in held])


def part(ref, start, size):
    return lambda: ref[start : start + size]


def lanes_at(index, size):
    return pl.ds(pl.multiple_of(index * size, size), size)


def along_tiles(operand, products, accs, target):
    def step(index, _):
        def job(tile, unit, at):
            def finish(*outs):
                for ref, out in zip(target, outs):
                    ref[tile] = out.reshape(16, 8, ROWS)

            return ([(lambda: operand(tile), True, products)], accs[unit][at % 2], finish)

        run([[job(index * UNROLL + 2 * at + unit, unit, at) for at in range(UNROLL // 2)] for unit in range(2)])
        return 0

    lax.fori_loop(0, PAIRS // UNROLL, step, 0)


def along_slow(source, target, op_ref, accs, add=None):
    def step(index, _):
        def job(block, unit, at):
            cache = []

            def high():
                cache.extend(split(source[:, block].reshape(256, ROWS)))
                return cache[0]

            def finish(out):
                out = out.reshape(PAIRS, 8, ROWS)
                target[:, block] = out if add is None else out + add[:, block]

            first = (high, False, [(0, part(op_ref, 0, 256)), (0, part(op_ref, 256, 256))])
            second = (lambda: cache[1], False, [(0, part(op_ref, 0, 256))])
            return ([first, second], [accs[unit][at % 2]], finish)

        run([[job(index * 8 + 2 * at + unit, unit, at) for at in range(4)] for unit in range(2)])
        return 0

    lax.fori_loop(0, 2, step, 0)


def natural(ref, index, pair):
    rows = []
    for tile in range(2):
        block = ref[index * 2 + tile, :, :, pair * 128 : pair * 128 + 128].reshape(8, 2, 8, 128)
        even, odd = block[:, 0], block[:, 1]
        upper = lax.broadcasted_iota(jnp.int32, even.shape, 1) < 4
        rows.append(jnp.where(upper, even, pltpu.roll(odd, 4, 1)).reshape(N, 128))
        rows.append(jnp.where(upper, pltpu.roll(even, 4, 1), odd).reshape(N, 128))
    return jnp.concatenate(rows, axis=0)


def along_x(steps_of, accs, finish_of, after):
    count = UNROLL // 2

    def step(index, _):
        def job(block, unit, at):
            return (steps_of(block, unit), [accs[unit][at % 2][0]], functools.partial(finish_of, block, unit))

        run([[job(index * count + at, unit, at) for at in range(count)] for unit in range(2)])
        if after is not None:
            for at in range(count):
                after(index * count + at)
        return 0

    lax.fori_loop(0, 16 // count, step, 0)


def chunks(core):
    for position in range(64):
        xh, xl, y, z = position // 32, position // 16 % 2, position // 4 % 4, position % 4
        member = xl * 4 + y
        plane = xh * 32 + z * 8 + member // 2
        yield position, plane + core * 4, plane + 4 - core * 4, member % 2


def forward_kernel(core_ref, occ_ref, z_ref, y_ref, x_ref, orb_ref, val_ref, keep_ref, send_ref, first, second, total, spread, *accs):
    group = pl.program_id(0)
    small, large = ((accs[0:1], accs[1:2]), (accs[2:3], accs[3:4])), (accs[4:6], accs[6:8])
    z_products = [(0, part(z_ref, 0, 128)), (0, part(z_ref, 128, 128))]
    x_products = [(0, part(x_ref, 0, 128)), (0, part(x_ref, 128, 128))]
    along_tiles(lambda tile: both(orb_ref[:, :, lanes_at(tile, 128)].reshape(ROWS, 128)), z_products, small, [first])
    along_slow(first, second, y_ref, large)

    @pl.when(group == 0)
    def _():
        total[...] = jnp.zeros_like(total)

    def finish(block, pair, out):
        lanes = lanes_at(block, 256)
        out = out.reshape(2, N, 256)
        val_ref[pair * 2 : pair * 2 + 2, :, lanes] = out
        weighted = [occ_ref[group * GROUP + pair * 2 + one] * (out[one] * out[one]) for one in range(2)]
        total[:, lanes] = total[:, lanes] + (weighted[0] + weighted[1])

    along_x(lambda block, pair: [(lambda: both(natural(second, block, pair)), True, x_products)], small, finish, None)

    @pl.when(group == pl.num_programs(0) - 1)
    def _():
        for tile in range(32):
            spread[pl.ds(tile, N, stride=32), :] = total[:, tile * 128 : tile * 128 + 128]
        for position, here, there, half in chunks(core_ref[0]):
            keep_ref[position] = spread[pl.ds(pl.multiple_of(here * 32 + half * 16, 16), 16), :]
            send_ref[position] = spread[pl.ds(pl.multiple_of(there * 32 + half * 16, 16), 16), :]


def back_kernel(core_ref, z_ref, y_ref, x_ref, own_ref, other_ref, val_ref, kin0_ref, kin1_ref, out_ref, first, second, total, spread, *accs):
    group = pl.program_id(0)
    small, large = ((accs[0:1], accs[1:2]), (accs[2:3], accs[3:4])), (accs[4:6], accs[6:8])
    z_products = [(0, part(z_ref, 0, 128)), (0, part(z_ref, 128, 128))]
    x_products = [(0, part(x_ref, 0, 128)), (0, part(x_ref, 128, 128))]

    @pl.when(group == 0)
    def _():
        for position, here, there, half in chunks(core_ref[0]):
            spread[pl.ds(pl.multiple_of(here * 32 + half * 16, 16), 16), :] = own_ref[position]
            spread[pl.ds(pl.multiple_of(there * 32 + half * 16, 16), 16), :] = other_ref[position]
        for tile in range(32):
            total[:, tile * 128 : tile * 128 + 128] = spread[pl.ds(tile, N, stride=32), :]

    def weighted(tile):
        lanes = lanes_at(tile, 128)
        return both((val_ref[:, :, lanes] * total[:, lanes][None]).reshape(ROWS, 128))

    along_tiles(weighted, z_products, small, [first])
    along_slow(first, second, y_ref, large)

    for which, kin_ref in enumerate((kin0_ref, kin1_ref)):

        @pl.when(group == which)
        def _():
            def finish(block, pair, out):
                at = (slice(pair * 2, pair * 2 + 2), slice(None), lanes_at(block, 256))
                out_ref[at] = out.reshape(2, N, 256) + kin_ref[at]

            along_x(lambda block, pair: [(lambda: both(natural(second, block, pair)), True, x_products)], small, finish, None)


def kinetic_kernel(_, z_ref, y_ref, x_ref, orb_ref, out_ref, first, second, *accs):
    small, large = ((accs[0:2], accs[2:4]), (accs[4:6], accs[6:8])), (accs[8:10], accs[10:12])
    z_products = [(0, part(z_ref, 0, 128)), (1, part(z_ref, 128, 128)), (1, part(z_ref, 256, 128))]
    one_products = [(0, part(x_ref, 0, 128))]
    x_products = [(0, part(x_ref, 128, 128)), (0, part(x_ref, 256, 128))]
    along_tiles(lambda tile: both(orb_ref[:, :, lanes_at(tile, 128)].reshape(ROWS, 128)), z_products, small, [first, second])
    along_slow(first, second, y_ref, large, second)

    def steps(block, pair):
        return [
            (lambda: both(natural(second, block, pair)), True, one_products),
            (lambda: both(natural(first, block, pair)), True, x_products),
        ]

    def finish(block, pair, out):
        at = (slice(pair * 2, pair * 2 + 2), slice(None), lanes_at(block, 256))
        out_ref[at] = out.reshape(2, N, 256) + CENTRE * orb_ref[at]

    along_x(steps, small, finish, None)


SMEM = pl.BlockSpec(memory_space=pltpu.SMEM)
ORBITALS = pl.BlockSpec((GROUP, N, N * N), lambda group: (group, 0, 0))
TURNED = pltpu.VMEM((PAIRS, 16, 8, ROWS), jnp.float32)
PLANES = pltpu.VMEM((N, N * N), jnp.float32)
SPREAD = pltpu.VMEM((N * 32, 128), jnp.float32)
HALF = jax.ShapeDtypeStruct((64, 16, 128), jnp.float32)
ONE_ROWS = lane_operator(ONE)[:128]


def scoped(kernel, accs):
    return lambda *refs: pl.run_scoped(functools.partial(kernel, *refs), *accs)


def accs_for(*counts):
    small, large = counts
    return [pltpu.ACC(unit)((128, 256), jnp.float32) for unit in range(2) for _ in range(small)] + [
        pltpu.ACC(unit)((256, 256), jnp.float32) for unit in range(2) for _ in range(large)
    ]


def whole(shape):
    return pl.BlockSpec(shape, lambda *_: (0,) * len(shape), pipeline_mode=pl.Buffered(1))


def cost(rows, bytes_accessed):
    return pl.CostEstimate(flops=rows * 2 * 256 * 256, bytes_accessed=bytes_accessed, transcendentals=0)


def constants(*tables):
    return [whole(table.shape) for table in tables], [jnp.asarray(table) for table in tables]


def forward(core, occupations, orbitals):
    count = orbitals.shape[0]
    specs, tables = constants(lane_operator(MAGIC, MIXED), slow_operator(MAGIC), lane_operator(MAGIC))
    return pl.pallas_call(
        scoped(forward_kernel, accs_for(2, 2)),
        grid=(count // GROUP,),
        in_specs=[SMEM, SMEM, *specs, ORBITALS],
        out_specs=[ORBITALS, whole(HALF.shape), whole(HALF.shape)],
        out_shape=[jax.ShapeDtypeStruct(orbitals.shape, jnp.float32), HALF, HALF],
        scratch_shapes=[TURNED, TURNED, PLANES, SPREAD],
        compiler_params=pltpu.CompilerParams(**PARAMS),
        cost_estimate=cost(57344, 18 * 2**20),
        name="forward",
    )(core, occupations, *tables, orbitals)


def back(core, own, other, values, kin0, kin1):
    count = values.shape[0]
    specs, tables = constants(lane_operator(MAGIC.T, MIXED), slow_operator(MAGIC.T), lane_operator(MAGIC.T))
    quad = whole((GROUP, N, N * N))
    return pl.pallas_call(
        scoped(back_kernel, accs_for(2, 2)),
        grid=(count // GROUP,),
        in_specs=[SMEM, *specs, whole(HALF.shape), whole(HALF.shape), ORBITALS, quad, quad],
        out_specs=ORBITALS,
        out_shape=jax.ShapeDtypeStruct(values.shape, jnp.float32),
        scratch_shapes=[TURNED, TURNED, PLANES, SPREAD],
        compiler_params=pltpu.CompilerParams(**PARAMS),
        cost_estimate=cost(57344, 26 * 2**20),
        name="back",
    )(core, *tables, own, other, values, kin0, kin1)


def kinetic(after, orbitals, group):
    block = (GROUP, N, N * N)
    z_table = np.concatenate([ONE_ROWS[MIXED], lane_operator(SIDES, np.arange(128)[MIXED])])
    x_table = np.concatenate([ONE_ROWS, lane_operator(SIDES)])
    specs, tables = constants(z_table, slow_operator(SIDES), x_table)
    return pl.pallas_call(
        scoped(kinetic_kernel, accs_for(4, 2)),
        grid=(1,),
        in_specs=[SMEM, *specs, pl.BlockSpec(block, lambda _: (group, 0, 0))],
        out_specs=pl.BlockSpec(block, lambda _: (0, 0, 0)),
        out_shape=jax.ShapeDtypeStruct(block, jnp.float32),
        scratch_shapes=[TURNED, TURNED],
        compiler_params=pltpu.CompilerParams(**PARAMS),
        cost_estimate=cost(49152, 9 * 2**20),
        name=f"kinetic{group}",
    )(after, *tables, orbitals)


SWAP = [(0, 1), (1, 0)]


def on_device(orbitals, occupations, external):
    core = lax.axis_index("core").astype(jnp.int32).reshape(1)
    member = lax.axis_index("xl") * 4 + lax.axis_index("y")
    own_external = lax.dynamic_index_in_dim(external.reshape(8, 16, 128), member, 0, keepdims=False)
    values, keep, send = forward(core, occupations, orbitals)
    partial = keep + lax.ppermute(send, "core", SWAP)
    partial, after = lax.optimization_barrier((partial, core))
    shares = lax.all_to_all(partial, CHIPS, 0, 0, tiled=True)
    shares, kin0 = lax.optimization_barrier((shares, kinetic(after, orbitals, 0)))
    density = jnp.sum(shares, axis=0)
    potential = own_external - jnp.cbrt(3.0 / math.pi * density)
    copies, after = lax.optimization_barrier((jnp.broadcast_to(potential[None], (64, 16, 128)), core))
    own = lax.all_to_all(copies, CHIPS, 0, 0, tiled=True)
    own, kin1 = lax.optimization_barrier((own, kinetic(after, orbitals, 1)))
    other = lax.ppermute(own, "core", SWAP)
    return back(core, own, other, values, kin0, kin1)


def solution(mesh):
    fine = Mesh(mesh.devices.reshape(2, 4, 2, 2, 4), AXES)
    orb = ("xh", "z", "core")
    return jax.shard_map(
        on_device,
        mesh=fine,
        in_specs=(P(AXES, None, None), P(AXES), P(orb, None)),
        out_specs=P(AXES, None, None),
        check_vma=False,
    )
```

```python
import functools
import math

import jax
import jax.numpy as jnp
import ml_dtypes
import numpy as np
from jax import lax
from jax.experimental import pallas as pl
from jax.experimental.pallas import tpu as pltpu
from jax.sharding import Mesh, PartitionSpec as P

MAGIC_TAPS = [
    8.433424733352934e-07,
    -1.290557201342061e-05,
    8.76298447621056e-05,
    -0.00030158038132690465,
    0.001747237136729939,
    -0.009420470302010804,
    0.023738214637249424,
    0.0612625895831208,
    0.9940415697834003,
    -0.06048952891969835,
    -0.021030251609303816,
    0.013372634148547948,
    -0.0034412814449349387,
    0.0004944322768868992,
    -5.185986881173433e-05,
    2.7273449291197967e-06,
]
KINETIC_HALF = [
    -3.55369228991319,
    2.2191465938911166,
    -0.615614146557007,
    0.23717805821538057,
    -0.08226639997421234,
    0.022070291884822554,
    -0.004097656893426338,
    0.00045167920287502236,
    -2.3982285245075998e-05,
    2.0904234952920368e-06,
    -3.7230763047369276e-07,
    -1.0585705549674146e-08,
    -5.8138798302825403e-11,
    2.7080049362631943e-13,
    -6.9244749406392e-18,
]
KINETIC_TAPS = KINETIC_HALF[:0:-1] + KINETIC_HALF
SPACING = 0.45

N = 64
GROUP = 4
ROWS = GROUP * N
PAIRS = N // 2
BF16 = ml_dtypes.bfloat16
AXES = ("xh", "z", "core", "xl", "y")
CHIPS = ("xh", "xl", "y", "z")
UNROLL = 16


def circulant(taps, offset):
    matrix = np.zeros((N, N), np.float32)
    for position, weight in enumerate(taps):
        for row in range(N):
            matrix[row, (row + position - offset) % N] += np.float32(weight)
    return matrix


def halves(matrix):
    high = matrix.astype(BF16)
    return high, (matrix - high.astype(np.float32)).astype(BF16)


MIXED = np.arange(128).reshape(2, 16, 4).transpose(1, 0, 2).reshape(128)


def lane_operator(matrix, order=slice(None)):
    return np.concatenate([np.concatenate([part, part], 1)[order] for part in halves(np.kron(np.eye(2, dtype=np.float32), matrix))])


def slow_operator(matrix):
    return np.concatenate(halves(np.kron(matrix, np.eye(4, dtype=np.float32))))


MAGIC = circulant(MAGIC_TAPS, 8)
KINETIC = circulant(KINETIC_TAPS, 14) * np.float32(-0.5 / (SPACING * SPACING))
CENTRE = float(np.float32(3.0) * KINETIC[0, 0])
SIDES = KINETIC - np.diag(np.diag(KINETIC))
ONE = np.eye(N, dtype=np.float32)


def split(block):
    high = block.astype(jnp.bfloat16)
    return high, (block - high.astype(jnp.float32)).astype(jnp.bfloat16)


def both(block):
    return jnp.concatenate(split(block), axis=1)


def run(jobs):
    queues = []
    for unit, queue in enumerate(jobs):
        steps = []
        for index, (parts, accs, finish) in enumerate(queue):
            for at, part in enumerate(parts):
                steps.append((part, accs, finish if at == len(parts) - 1 else None))
        queues.append(steps)
    pending = [None] * len(queues)

    def push(unit, at):
        (operand, transpose, _), _, _ = queues[unit][at]
        pltpu.matmul_push_rhs(operand(), at % 2, unit, transpose=transpose)

    for unit in range(len(queues)):
        push(unit, 0)
    for at in range(len(queues[0])):
        for unit, queue in enumerate(queues):
            if at + 1 < len(queue):
                push(unit, at + 1)
            (_, _, products), accs, finish = queue[at]
            for which, (acc, left) in enumerate(products):
                pltpu.matmul_acc_lhs(accs[acc], left(), load_staged_rhs=at % 2 if which == 0 else None)
            if pending[unit] is not None:
                done, held = pending[unit]
                done(*[pltpu.matmul_pop(acc) for acc in held])
                pending[unit] = None
            if finish is not None:
                pending[unit] = (finish, accs)
    for done, held in pending:
        done(*[pltpu.matmul_pop(acc) for acc in held])


def part(ref, start, size):
    return lambda: ref[start : start + size]


def lanes_at(index, size):
    return pl.ds(pl.multiple_of(index * size, size), size)


def along_tiles(operand, products, accs, target, before):
    def step(index, _):
        before(index)

        def job(tile, unit, at):
            def finish(*outs):
                for ref, out in zip(target, outs):
                    ref[tile] = out.reshape(16, 8, ROWS)

            return ([(lambda: operand(tile), True, products)], accs[unit][at % 2], finish)

        run([[job(index * UNROLL + 2 * at + unit, unit, at) for at in range(UNROLL // 2)] for unit in range(2)])
        return 0

    lax.fori_loop(0, PAIRS // UNROLL, step, 0)


def along_slow(source, target, op_ref, accs, add=None):
    def step(index, _):
        def job(block, unit, at):
            cache = []

            def high():
                cache.extend(split(source[:, block].reshape(256, ROWS)))
                return cache[0]

            def finish(out):
                out = out.reshape(PAIRS, 8, ROWS)
                target[:, block] = out if add is None else out + add[:, block]

            first = (high, False, [(0, part(op_ref, 0, 256)), (0, part(op_ref, 256, 256))])
            second = (lambda: cache[1], False, [(0, part(op_ref, 0, 256))])
            return ([first, second], [accs[unit][at % 2]], finish)

        run([[job(index * 8 + 2 * at + unit, unit, at) for at in range(4)] for unit in range(2)])
        return 0

    lax.fori_loop(0, 2, step, 0)


def natural(ref, index, pair):
    rows = []
    for tile in range(2):
        block = ref[index * 2 + tile, :, :, pair * 128 : pair * 128 + 128].reshape(8, 2, 8, 128)
        even, odd = block[:, 0], block[:, 1]
        upper = lax.broadcasted_iota(jnp.int32, even.shape, 1) < 4
        rows.append(jnp.where(upper, even, pltpu.roll(odd, 4, 1)).reshape(N, 128))
        rows.append(jnp.where(upper, pltpu.roll(even, 4, 1), odd).reshape(N, 128))
    return jnp.concatenate(rows, axis=0)


def along_x(steps_of, accs, finish_of, before, after):
    count = UNROLL // 2

    def step(index, _):
        before(index)

        def job(block, unit, at):
            return (steps_of(block, unit), [accs[unit][at % 2][0]], functools.partial(finish_of, block, unit))

        run([[job(index * count + at, unit, at) for at in range(count)] for unit in range(2)])
        after(index)
        return 0

    lax.fori_loop(0, 16 // count, step, 0)


def piece(group, index):
    return (pl.ds(group * GROUP, GROUP), slice(None), lanes_at(index, UNROLL * 128))


def nothing(_):
    return None


def chunks(core):
    for position in range(64):
        xh, xl, y, z = position // 32, position // 16 % 2, position // 4 % 4, position % 4
        member = xl * 4 + y
        plane = xh * 32 + z * 8 + member // 2
        yield position, plane + core * 4, plane + 4 - core * 4, member % 2


def forward_kernel(core_ref, occ_ref, z_ref, y_ref, x_ref, orb_hbm, val_hbm, keep_ref, send_ref, orbs, first, second, total, spread, arrived, left, *accs):
    small, large = ((accs[0:1], accs[1:2]), (accs[2:3], accs[3:4])), (accs[4:6], accs[6:8])
    z_products = [(0, part(z_ref, 0, 128)), (0, part(z_ref, 128, 128))]
    x_products = [(0, part(x_ref, 0, 128)), (0, part(x_ref, 128, 128))]

    def fetch(group, index):
        return pltpu.make_async_copy(orb_hbm.at[piece(group, index)], orbs.at[piece(group, index)], arrived.at[group, index])

    def give(group, index):
        return pltpu.make_async_copy(orbs.at[piece(group, index)], val_hbm.at[piece(group, index)], left.at[group, index])

    fetch(0, 0).start()
    fetch(0, 1).start()
    total[...] = jnp.zeros_like(total)

    def one_group(group, _):
        mine = orbs.at[pl.ds(group * GROUP, GROUP)]

        def before(index):
            fetch(group, index).wait()

            @pl.when(group == 0)
            def _():
                fetch(1, index).start()

        along_tiles(lambda tile: both(mine[:, :, lanes_at(tile, 128)].reshape(ROWS, 128)), z_products, small, [first], before)
        along_slow(first, second, y_ref, large)

        def finish(block, pair, out):
            lanes = lanes_at(block, 256)
            out = out.reshape(2, N, 256)
            mine[pair * 2 : pair * 2 + 2, :, lanes] = out
            weighted = [occ_ref[group * GROUP + pair * 2 + one] * (out[one] * out[one]) for one in range(2)]
            total[:, lanes] = total[:, lanes] + (weighted[0] + weighted[1])

        steps = lambda block, pair: [(lambda: both(natural(second, block, pair)), True, x_products)]
        along_x(steps, small, finish, nothing, lambda index: give(group, index).start())
        return 0

    lax.fori_loop(0, 2, one_group, 0)
    for tile in range(32):
        spread[pl.ds(tile, N, stride=32), :] = total[:, tile * 128 : tile * 128 + 128]
    for position, here, there, half in chunks(core_ref[0]):
        keep_ref[position] = spread[pl.ds(pl.multiple_of(here * 32 + half * 16, 16), 16), :]
        send_ref[position] = spread[pl.ds(pl.multiple_of(there * 32 + half * 16, 16), 16), :]
    for group in range(2):
        for index in range(2):
            give(group, index).wait()


def back_kernel(core_ref, z_ref, y_ref, x_ref, own_hbm, other_hbm, val_hbm, kin0_hbm, kin1_hbm, out_hbm, vals, kins, first, second, total, spread, own, other, arrived, kin_arrived, left, halves_arrived, *accs):
    small, large = ((accs[0:1], accs[1:2]), (accs[2:3], accs[3:4])), (accs[4:6], accs[6:8])
    z_products = [(0, part(z_ref, 0, 128)), (0, part(z_ref, 128, 128))]
    x_products = [(0, part(x_ref, 0, 128)), (0, part(x_ref, 128, 128))]

    def fetch(group, index):
        return pltpu.make_async_copy(val_hbm.at[piece(group, index)], vals.at[piece(group, index)], arrived.at[group, index])

    def fetch_kin(which, index):
        source = (kin0_hbm, kin1_hbm)[which]
        return pltpu.make_async_copy(source.at[piece(0, index)], kins.at[piece(which, index)], kin_arrived.at[which, index])

    def give(group, index):
        return pltpu.make_async_copy(vals.at[piece(group, index)], out_hbm.at[piece(group, index)], left.at[group, index])

    pots = [pltpu.make_async_copy(source, target, halves_arrived.at[at]) for at, (source, target) in enumerate(((own_hbm, own), (other_hbm, other)))]
    for copy in pots:
        copy.start()
    fetch(0, 0).start()
    fetch(0, 1).start()
    for copy in pots:
        copy.wait()
    for position, here, there, half in chunks(core_ref[0]):
        spread[pl.ds(pl.multiple_of(here * 32 + half * 16, 16), 16), :] = own[position]
        spread[pl.ds(pl.multiple_of(there * 32 + half * 16, 16), 16), :] = other[position]
    for tile in range(32):
        total[:, tile * 128 : tile * 128 + 128] = spread[pl.ds(tile, N, stride=32), :]

    def one_group(group, _):
        mine, kin = vals.at[pl.ds(group * GROUP, GROUP)], kins.at[pl.ds(group * GROUP, GROUP)]

        def before(index):
            fetch(group, index).wait()
            for which in range(2):

                @pl.when(group == which)
                def _():
                    fetch_kin(which, index).start()
                    if which == 0:
                        fetch(1, index).start()

        def weighted(tile):
            lanes = lanes_at(tile, 128)
            return both((mine[:, :, lanes] * total[:, lanes][None]).reshape(ROWS, 128))

        along_tiles(weighted, z_products, small, [first], before)
        along_slow(first, second, y_ref, large)

        def finish(block, pair, out):
            at = (slice(pair * 2, pair * 2 + 2), slice(None), lanes_at(block, 256))
            mine[at] = out.reshape(2, N, 256) + kin[at]

        def before_x(index):
            for which in range(2):

                @pl.when(group == which)
                def _():
                    fetch_kin(which, index).wait()

        steps = lambda block, pair: [(lambda: both(natural(second, block, pair)), True, x_products)]
        along_x(steps, small, finish, before_x, lambda index: give(group, index).start())
        return 0

    lax.fori_loop(0, 2, one_group, 0)
    for group in range(2):
        for index in range(2):
            give(group, index).wait()


def kinetic_kernel(group, _, z_ref, y_ref, x_ref, orb_hbm, out_hbm, orbs, first, second, arrived, left, *accs):
    small, large = ((accs[0:2], accs[2:4]), (accs[4:6], accs[6:8])), (accs[8:10], accs[10:12])
    z_products = [(0, part(z_ref, 0, 128)), (1, part(z_ref, 128, 128)), (1, part(z_ref, 256, 128))]
    one_products = [(0, part(x_ref, 0, 128))]
    x_products = [(0, part(x_ref, 128, 128)), (0, part(x_ref, 256, 128))]

    def fetch(index):
        return pltpu.make_async_copy(orb_hbm.at[piece(group, index)], orbs.at[piece(0, index)], arrived.at[index])

    def give(index):
        return pltpu.make_async_copy(orbs.at[piece(0, index)], out_hbm.at[piece(0, index)], left.at[index])

    fetch(0).start()
    fetch(1).start()
    operand = lambda tile: both(orbs[:, :, lanes_at(tile, 128)].reshape(ROWS, 128))
    along_tiles(operand, z_products, small, [first, second], lambda index: fetch(index).wait())
    along_slow(first, second, y_ref, large, second)

    def steps(block, pair):
        return [
            (lambda: both(natural(second, block, pair)), True, one_products),
            (lambda: both(natural(first, block, pair)), True, x_products),
        ]

    def finish(block, pair, out):
        at = (slice(pair * 2, pair * 2 + 2), slice(None), lanes_at(block, 256))
        orbs[at] = out.reshape(2, N, 256) + CENTRE * orbs[at]

    along_x(steps, small, finish, nothing, lambda index: give(index).start())
    give(0).wait()
    give(1).wait()


SMEM = pl.BlockSpec(memory_space=pltpu.SMEM)
ANY = pl.BlockSpec(memory_space=pl.ANY)
HBM = pl.BlockSpec(memory_space=pltpu.HBM)
ALL = pltpu.VMEM((2 * GROUP, N, N * N), jnp.float32)
QUAD = pltpu.VMEM((GROUP, N, N * N), jnp.float32)
TURNED = pltpu.VMEM((PAIRS, 16, 8, ROWS), jnp.float32)
PLANES = pltpu.VMEM((N, N * N), jnp.float32)
SPREAD = pltpu.VMEM((N * 32, 128), jnp.float32)
HALF = jax.ShapeDtypeStruct((64, 16, 128), jnp.float32)
ONE_ROWS = lane_operator(ONE)[:128]


def scoped(kernel, accs):
    return lambda *refs: pl.run_scoped(functools.partial(kernel, *refs), *accs)


def accs_for(*counts):
    small, large = counts
    return [pltpu.ACC(unit)((128, 256), jnp.float32) for unit in range(2) for _ in range(small)] + [
        pltpu.ACC(unit)((256, 256), jnp.float32) for unit in range(2) for _ in range(large)
    ]


def whole(shape):
    return pl.BlockSpec(shape, lambda *_: (0,) * len(shape))


def cost(rows, bytes_accessed):
    return pl.CostEstimate(flops=rows * 2 * 256 * 256, bytes_accessed=bytes_accessed, transcendentals=0)


def constants(*tables):
    return [whole(table.shape) for table in tables], [jnp.asarray(table) for table in tables]


def sems(*shape):
    return pltpu.SemaphoreType.DMA(shape)


def params(mib):
    return pltpu.CompilerParams(vmem_limit_bytes=mib * 2**20)


def forward(core, occupations, orbitals):
    specs, tables = constants(lane_operator(MAGIC, MIXED), slow_operator(MAGIC), lane_operator(MAGIC))
    return pl.pallas_call(
        scoped(forward_kernel, accs_for(2, 2)),
        in_specs=[SMEM, SMEM, *specs, HBM],
        out_specs=[HBM, whole(HALF.shape), whole(HALF.shape)],
        out_shape=[jax.ShapeDtypeStruct(orbitals.shape, jnp.float32), HALF, HALF],
        scratch_shapes=[ALL, TURNED, TURNED, PLANES, SPREAD, sems(2, 2), sems(2, 2)],
        compiler_params=params(52),
        cost_estimate=cost(57344, 18 * 2**20),
        name="forward",
    )(core, occupations, *tables, orbitals)


def back(core, own, other, values, kin0, kin1):
    specs, tables = constants(lane_operator(MAGIC.T, MIXED), slow_operator(MAGIC.T), lane_operator(MAGIC.T))
    half = pltpu.VMEM(HALF.shape, jnp.float32)
    return pl.pallas_call(
        scoped(back_kernel, accs_for(2, 2)),
        in_specs=[SMEM, *specs, ANY, ANY, HBM, HBM, HBM],
        out_specs=HBM,
        out_shape=jax.ShapeDtypeStruct(values.shape, jnp.float32),
        scratch_shapes=[ALL, ALL, TURNED, TURNED, PLANES, SPREAD, half, half, sems(2, 2), sems(2, 2), sems(2, 2), sems(2)],
        compiler_params=params(52),
        cost_estimate=cost(57344, 26 * 2**20),
        name="back",
    )(core, *tables, own, other, values, kin0, kin1)


def kinetic(after, orbitals, group):
    z_table = np.concatenate([ONE_ROWS[MIXED], lane_operator(SIDES, MIXED)])
    x_table = np.concatenate([ONE_ROWS, lane_operator(SIDES)])
    specs, tables = constants(z_table, slow_operator(SIDES), x_table)
    return pl.pallas_call(
        scoped(functools.partial(kinetic_kernel, group), accs_for(4, 2)),
        in_specs=[SMEM, *specs, HBM],
        out_specs=HBM,
        out_shape=jax.ShapeDtypeStruct((GROUP, N, N * N), jnp.float32),
        scratch_shapes=[QUAD, TURNED, TURNED, sems(2), sems(2)],
        compiler_params=params(52),
        cost_estimate=cost(49152, 9 * 2**20),
        name=f"kinetic{group}",
    )(after, *tables, orbitals)


SWAP = [(0, 1), (1, 0)]


def on_device(orbitals, occupations, external):
    core = lax.axis_index("core").astype(jnp.int32).reshape(1)
    member = lax.axis_index("xl") * 4 + lax.axis_index("y")
    own_external = lax.dynamic_index_in_dim(external.reshape(8, 16, 128), member, 0, keepdims=False)
    values, keep, send = forward(core, occupations, orbitals)
    partial = keep + lax.ppermute(send, "core", SWAP)
    partial, after = lax.optimization_barrier((partial, core))
    shares = lax.all_to_all(partial, CHIPS, 0, 0, tiled=True)
    shares, kin0 = lax.optimization_barrier((shares, kinetic(after, orbitals, 0)))
    density = jnp.sum(shares, axis=0)
    potential = own_external - jnp.cbrt(3.0 / math.pi * density)
    copies, after = lax.optimization_barrier((jnp.broadcast_to(potential[None], (64, 16, 128)), core))
    own = lax.all_to_all(copies, CHIPS, 0, 0, tiled=True)
    own, kin1 = lax.optimization_barrier((own, kinetic(after, orbitals, 1)))
    other = lax.ppermute(own, "core", SWAP)
    return back(core, own, other, values, kin0, kin1)


def solution(mesh):
    fine = Mesh(mesh.devices.reshape(2, 4, 2, 2, 4), AXES)
    orb = ("xh", "z", "core")
    return jax.shard_map(
        on_device,
        mesh=fine,
        in_specs=(P(AXES, None, None), P(AXES), P(orb, None)),
        out_specs=P(AXES, None, None),
        check_vma=False,
    )
```

```python
import functools
import math

import jax
import jax.numpy as jnp
import ml_dtypes
import numpy as np
from jax import lax
from jax.experimental import pallas as pl
from jax.experimental.pallas import tpu as pltpu
from jax.sharding import Mesh, PartitionSpec as P

MAGIC_TAPS = [
    8.433424733352934e-07,
    -1.290557201342061e-05,
    8.76298447621056e-05,
    -0.00030158038132690465,
    0.001747237136729939,
    -0.009420470302010804,
    0.023738214637249424,
    0.0612625895831208,
    0.9940415697834003,
    -0.06048952891969835,
    -0.021030251609303816,
    0.013372634148547948,
    -0.0034412814449349387,
    0.0004944322768868992,
    -5.185986881173433e-05,
    2.7273449291197967e-06,
]
KINETIC_HALF = [
    -3.55369228991319,
    2.2191465938911166,
    -0.615614146557007,
    0.23717805821538057,
    -0.08226639997421234,
    0.022070291884822554,
    -0.004097656893426338,
    0.00045167920287502236,
    -2.3982285245075998e-05,
    2.0904234952920368e-06,
    -3.7230763047369276e-07,
    -1.0585705549674146e-08,
    -5.8138798302825403e-11,
    2.7080049362631943e-13,
    -6.9244749406392e-18,
]
KINETIC_TAPS = KINETIC_HALF[:0:-1] + KINETIC_HALF
SPACING = 0.45

N = 64
GROUP = 4
ROWS = GROUP * N
PAIRS = N // 2
BF16 = ml_dtypes.bfloat16
AXES = ("xh", "z", "core", "xl", "y")
CHIPS = ("xh", "xl", "y", "z")
PIECES = 2


def circulant(taps, offset):
    matrix = np.zeros((N, N), np.float32)
    for position, weight in enumerate(taps):
        for row in range(N):
            matrix[row, (row + position - offset) % N] += np.float32(weight)
    return matrix


def halves(matrix):
    high = matrix.astype(BF16)
    return high, (matrix - high.astype(np.float32)).astype(BF16)


MIXED = np.arange(128).reshape(2, 16, 4).transpose(1, 0, 2).reshape(128)


def lane_operator(matrix, order=slice(None)):
    return np.concatenate([np.concatenate([part, part], 1)[order] for part in halves(np.kron(np.eye(2, dtype=np.float32), matrix))])


def slow_operator(matrix):
    return np.concatenate(halves(np.kron(matrix, np.eye(4, dtype=np.float32))))


MAGIC = circulant(MAGIC_TAPS, 8)
KINETIC = circulant(KINETIC_TAPS, 14) * np.float32(-0.5 / (SPACING * SPACING))
CENTRE = float(np.float32(3.0) * KINETIC[0, 0])
SIDES = KINETIC - np.diag(np.diag(KINETIC))
ONE = np.eye(N, dtype=np.float32)


def split(block):
    high = block.astype(jnp.bfloat16)
    return high, (block - high.astype(jnp.float32)).astype(jnp.bfloat16)


def both(block):
    return jnp.concatenate(split(block), axis=1)


def run(jobs):
    queues = []
    for unit, queue in enumerate(jobs):
        steps = []
        for index, (parts, accs, finish) in enumerate(queue):
            for at, part in enumerate(parts):
                steps.append((part, accs, finish if at == len(parts) - 1 else None))
        queues.append(steps)
    pending = [None] * len(queues)

    def push(unit, at):
        (operand, transpose, _), _, _ = queues[unit][at]
        pltpu.matmul_push_rhs(operand(), at % 2, unit, transpose=transpose)

    for unit in range(len(queues)):
        push(unit, 0)
    for at in range(len(queues[0])):
        for unit, queue in enumerate(queues):
            if at + 1 < len(queue):
                push(unit, at + 1)
            (_, _, products), accs, finish = queue[at]
            for which, (acc, left) in enumerate(products):
                pltpu.matmul_acc_lhs(accs[acc], left(), load_staged_rhs=at % 2 if which == 0 else None)
            if pending[unit] is not None:
                done, held = pending[unit]
                done(*[pltpu.matmul_pop(acc) for acc in held])
                pending[unit] = None
            if finish is not None:
                pending[unit] = (finish, accs)
    for done, held in pending:
        done(*[pltpu.matmul_pop(acc) for acc in held])


def part(ref, start, size):
    return lambda: ref[start : start + size]


def lanes_at(index, size):
    return pl.ds(pl.multiple_of(index * size, size), size)


def repeat(count, body):
    if count == 1:
        body(0)
    else:

        def step(index, _):
            body(index)
            return 0

        lax.fori_loop(0, count, step, 0)


def along_tiles(loops, operand, products, accs, target, before):
    count = PAIRS // loops // 2

    def body(index):
        before(index)

        def job(tile, unit, at):
            def finish(*outs):
                for ref, out in zip(target, outs):
                    ref[tile] = out.reshape(16, 8, ROWS)

            return ([(lambda: operand(tile), True, products)], accs[unit][at % 2], finish)

        run([[job((index * count + at) * 2 + unit, unit, at) for at in range(count)] for unit in range(2)])

    repeat(loops, body)


def along_slow(loops, source, target, op_ref, accs, add=None):
    count = 8 // loops

    def body(index):
        def job(block, unit, at):
            cache = []

            def high():
                cache.extend(split(source[:, block].reshape(256, ROWS)))
                return cache[0]

            def finish(out):
                out = out.reshape(PAIRS, 8, ROWS)
                target[:, block] = out if add is None else out + add[:, block]

            first = (high, False, [(0, part(op_ref, 0, 256)), (0, part(op_ref, 256, 256))])
            second = (lambda: cache[1], False, [(0, part(op_ref, 0, 256))])
            return ([first, second], [accs[unit][at % 2]], finish)

        run([[job((index * count + at) * 2 + unit, unit, at) for at in range(count)] for unit in range(2)])

    repeat(loops, body)


def natural(ref, index, pair):
    rows = []
    for tile in range(2):
        block = ref[index * 2 + tile, :, :, pair * 128 : pair * 128 + 128].reshape(8, 2, 8, 128)
        even, odd = block[:, 0], block[:, 1]
        upper = lax.broadcasted_iota(jnp.int32, even.shape, 1) < 4
        rows.append(jnp.where(upper, even, pltpu.roll(odd, 4, 1)).reshape(N, 128))
        rows.append(jnp.where(upper, pltpu.roll(even, 4, 1), odd).reshape(N, 128))
    return jnp.concatenate(rows, axis=0)


def along_x(loops, steps_of, accs, finish_of, before, after):
    count = 16 // loops

    def body(index):
        before(index)

        def job(block, unit, at):
            return (steps_of(block, unit), [accs[unit][at % 2][0]], functools.partial(finish_of, block, unit))

        run([[job(index * count + at, unit, at) for at in range(count)] for unit in range(2)])
        after(index)

    repeat(loops, body)


def nothing(_):
    return None


def piece(group, index):
    return (pl.ds(group * GROUP, GROUP), slice(None), lanes_at(index, N * N // PIECES))


def places():
    for position in range(64):
        xh, xl, y, z = position // 32, position // 16 % 2, position // 4 % 4, position % 4
        for pair in range(2):
            yield position, (xh * 4 + z) * 8, (xl * 4 + y) * 4 + pair * 2, pair * 8


def exchange_halves(low, high):
    upper = lax.broadcasted_iota(jnp.int32, low.shape, 0) < 4
    return jnp.where(upper, low, pltpu.roll(high, 4, 0)), jnp.where(upper, pltpu.roll(low, 4, 0), high)


def forward_kernel(core_ref, occ_hbm, z_hbm, y_hbm, x_hbm, orb_hbm, val_hbm, keep_ref, send_ref, occ_ref, z_ref, y_ref, x_ref, orbs, first, second, total, ready, arrived, left, *accs):
    small, large = ((accs[0:1], accs[1:2]), (accs[2:3], accs[3:4])), (accs[4:6], accs[6:8])
    z_products = [(0, part(z_ref, 0, 128)), (0, part(z_ref, 128, 128))]
    x_products = [(0, part(x_ref, 0, 128)), (0, part(x_ref, 128, 128))]

    def fetch(group, index):
        return pltpu.make_async_copy(orb_hbm.at[piece(group, index)], orbs.at[piece(group, index)], arrived.at[group, index])

    def give(group, index):
        return pltpu.make_async_copy(orbs.at[piece(group, index)], val_hbm.at[piece(group, index)], left.at[group, index])

    tables = [
        pltpu.make_async_copy(source, target, ready.at[at])
        for at, (source, target) in enumerate(((z_hbm, z_ref), (y_hbm, y_ref), (x_hbm, x_ref), (occ_hbm, occ_ref)))
    ]
    tables[0].start()
    fetch(0, 0).start()
    fetch(0, 1).start()
    for table in tables[1:]:
        table.start()
    total[...] = jnp.zeros_like(total)
    tables[0].wait()

    def one_group(group, _):
        mine = orbs.at[pl.ds(group * GROUP, GROUP)]

        def before(index):
            fetch(group, index).wait()

            @pl.when(group == 0)
            def _():
                fetch(1, index).start()

        def operand(tile):
            return both(mine[:, :, lanes_at(tile, 128)].reshape(ROWS, 128))

        along_tiles(2, operand, z_products, small, [first], before)

        @pl.when(group == 0)
        def _():
            for table in tables[1:]:
                table.wait()

        along_slow(1, first, second, y_ref, large)

        def finish(block, pair, out):
            lanes = lanes_at(block, 256)
            out = out.reshape(2, N, 256)
            mine[pair * 2 : pair * 2 + 2, :, lanes] = out
            weighted = [occ_ref[group * GROUP + pair * 2 + one] * (out[one] * out[one]) for one in range(2)]
            total[:, lanes] = total[:, lanes] + (weighted[0] + weighted[1])

        along_x(2, lambda block, pair: [(lambda: both(natural(second, block, pair)), True, x_products)], small, finish, nothing, lambda index: give(group, index).start())
        return 0

    lax.fori_loop(0, 2, one_group, 0)
    core = core_ref[0]
    for position, row, tile, at in places():
        low, high = [total[row : row + 8, one * 128 : one * 128 + 128] for one in (tile, tile + 1)]
        zero, one = exchange_halves(low, high)
        keep_ref[position, at : at + 8, :] = jnp.where(core == 0, zero, one)
        send_ref[position, at : at + 8, :] = jnp.where(core == 0, one, zero)
    for group in range(2):
        for index in range(PIECES):
            give(group, index).wait()


def back_kernel(core_ref, z_hbm, y_hbm, x_hbm, own_hbm, other_hbm, val_hbm, kin0_hbm, kin1_hbm, out_hbm, z_ref, y_ref, x_ref, vals, kins, first, second, total, own, other, ready, arrived, kin_arrived, left, halves_arrived, *accs):
    small, large = ((accs[0:1], accs[1:2]), (accs[2:3], accs[3:4])), (accs[4:6], accs[6:8])
    z_products = [(0, part(z_ref, 0, 128)), (0, part(z_ref, 128, 128))]
    x_products = [(0, part(x_ref, 0, 128)), (0, part(x_ref, 128, 128))]

    def fetch(group, index):
        return pltpu.make_async_copy(val_hbm.at[piece(group, index)], vals.at[piece(group, index)], arrived.at[group, index])

    def fetch_kin(which, index):
        source = (kin0_hbm, kin1_hbm)[which]
        return pltpu.make_async_copy(source.at[piece(0, index)], kins.at[piece(which, index)], kin_arrived.at[which, index])

    def give(group, index):
        return pltpu.make_async_copy(vals.at[piece(group, index)], out_hbm.at[piece(group, index)], left.at[group, index])

    pots = [pltpu.make_async_copy(source, target, halves_arrived.at[at]) for at, (source, target) in enumerate(((own_hbm, own), (other_hbm, other)))]
    tables = [
        pltpu.make_async_copy(source, target, ready.at[at]) for at, (source, target) in enumerate(((z_hbm, z_ref), (y_hbm, y_ref), (x_hbm, x_ref)))
    ]
    for copy in pots + tables[:1]:
        copy.start()
    fetch(0, 0).start()
    fetch(0, 1).start()
    for copy in tables[1:]:
        copy.start()
    for copy in pots:
        copy.wait()
    core = core_ref[0]
    for position, row, tile, at in places():
        mine, theirs = own[position, at : at + 8, :], other[position, at : at + 8, :]
        low, high = exchange_halves(jnp.where(core == 0, mine, theirs), jnp.where(core == 0, theirs, mine))
        total[row : row + 8, tile * 128 : tile * 128 + 128] = low
        total[row : row + 8, tile * 128 + 128 : tile * 128 + 256] = high
    tables[0].wait()

    def one_group(group, _):
        mine, kin = vals.at[pl.ds(group * GROUP, GROUP)], kins.at[pl.ds(group * GROUP, GROUP)]

        def before(index):
            fetch(group, index).wait()

            @pl.when((group == 0) & (index == 0))
            def _():
                fetch_kin(0, 0).start()
                fetch_kin(0, 1).start()

            @pl.when((group == 0) & (index == 1))
            def _():
                fetch(1, 0).start()
                fetch(1, 1).start()

        def operand(tile):
            lanes = lanes_at(tile, 128)
            return both((mine[:, :, lanes] * total[:, lanes][None]).reshape(ROWS, 128))

        along_tiles(2, operand, z_products, small, [first], before)

        @pl.when(group == 0)
        def _():
            for table in tables[1:]:
                table.wait()

        along_slow(1, first, second, y_ref, large)

        def before_x(index):
            for which in range(2):

                @pl.when(group == which)
                def _():
                    fetch_kin(which, index).wait()
                    if which == 0:
                        fetch_kin(1, index).start()

        def finish(block, pair, out):
            at = (slice(pair * 2, pair * 2 + 2), slice(None), lanes_at(block, 256))
            mine[at] = out.reshape(2, N, 256) + kin[at]

        along_x(2, lambda block, pair: [(lambda: both(natural(second, block, pair)), True, x_products)], small, finish, before_x, lambda index: give(group, index).start())
        return 0

    lax.fori_loop(0, 2, one_group, 0)
    for group in range(2):
        for index in range(PIECES):
            give(group, index).wait()


def kinetic_kernel(group, _, z_ref, y_ref, x_ref, orb_hbm, out_hbm, orbs, first, second, arrived, left, *accs):
    small, large = ((accs[0:2], accs[2:4]), (accs[4:6], accs[6:8])), (accs[8:10], accs[10:12])
    z_products = [(0, part(z_ref, 0, 128)), (1, part(z_ref, 128, 128)), (1, part(z_ref, 256, 128))]
    one_products = [(0, part(x_ref, 0, 128))]
    x_products = [(0, part(x_ref, 128, 128)), (0, part(x_ref, 256, 128))]
    def fetch(index):
        return pltpu.make_async_copy(orb_hbm.at[piece(group, index)], orbs.at[piece(0, index)], arrived.at[index])

    def give(index):
        return pltpu.make_async_copy(orbs.at[piece(0, index)], out_hbm.at[piece(0, index)], left.at[index])

    fetch(0).start()
    fetch(1).start()
    operand = lambda tile: both(orbs[:, :, lanes_at(tile, 128)].reshape(ROWS, 128))
    along_tiles(2, operand, z_products, small, [first, second], lambda index: fetch(index).wait())
    along_slow(1, first, second, y_ref, large, second)

    def steps(block, pair):
        return [
            (lambda: both(natural(second, block, pair)), True, one_products),
            (lambda: both(natural(first, block, pair)), True, x_products),
        ]

    def finish(block, pair, out):
        at = (slice(pair * 2, pair * 2 + 2), slice(None), lanes_at(block, 256))
        orbs[at] = out.reshape(2, N, 256) + CENTRE * orbs[at]

    along_x(2, steps, small, finish, nothing, lambda index: give(index).start())
    give(0).wait()
    give(1).wait()


SMEM = pl.BlockSpec(memory_space=pltpu.SMEM)
ANY = pl.BlockSpec(memory_space=pl.ANY)
HBM = pl.BlockSpec(memory_space=pltpu.HBM)
ALL = pltpu.VMEM((2 * GROUP, N, N * N), jnp.float32)
QUAD = pltpu.VMEM((GROUP, N, N * N), jnp.float32)
TURNED = pltpu.VMEM((PAIRS, 16, 8, ROWS), jnp.float32)
PLANES = pltpu.VMEM((N, N * N), jnp.float32)
HALF = jax.ShapeDtypeStruct((64, 16, 128), jnp.float32)
ONE_ROWS = lane_operator(ONE)[:128]


def scoped(kernel, accs):
    return lambda *refs: pl.run_scoped(functools.partial(kernel, *refs), *accs)


def accs_for(*counts):
    small, large = counts
    return [pltpu.ACC(unit)((128, 256), jnp.float32) for unit in range(2) for _ in range(small)] + [
        pltpu.ACC(unit)((256, 256), jnp.float32) for unit in range(2) for _ in range(large)
    ]


def whole(shape):
    return pl.BlockSpec(shape, lambda *_: (0,) * len(shape))


def cost(rows, bytes_accessed):
    return pl.CostEstimate(flops=rows * 2 * 256 * 256, bytes_accessed=bytes_accessed, transcendentals=0)


TABLES = [pltpu.VMEM((256, 256), jnp.bfloat16), pltpu.VMEM((512, 256), jnp.bfloat16), pltpu.VMEM((256, 256), jnp.bfloat16)]


def constants(*tables):
    return [whole(table.shape) for table in tables], [jnp.asarray(table) for table in tables]


def sems(*shape):
    return pltpu.SemaphoreType.DMA(shape)


def params(mib):
    return pltpu.CompilerParams(vmem_limit_bytes=mib * 2**20)


def forward(core, occupations, orbitals):
    _, tables = constants(lane_operator(MAGIC, MIXED), slow_operator(MAGIC), lane_operator(MAGIC))
    return pl.pallas_call(
        scoped(forward_kernel, accs_for(2, 2)),
        in_specs=[SMEM, ANY, ANY, ANY, ANY, HBM],
        out_specs=[HBM, whole(HALF.shape), whole(HALF.shape)],
        out_shape=[jax.ShapeDtypeStruct(orbitals.shape, jnp.float32), HALF, HALF],
        scratch_shapes=[pltpu.SMEM((2 * GROUP,), jnp.float32), *TABLES, ALL, TURNED, TURNED, PLANES, sems(4), sems(2, PIECES), sems(2, PIECES)],
        compiler_params=params(60),
        cost_estimate=cost(57344, 18 * 2**20),
        name="forward",
    )(core, occupations, *tables, orbitals)


def back(core, own, other, values, kin0, kin1):
    _, tables = constants(lane_operator(MAGIC.T, MIXED), slow_operator(MAGIC.T), lane_operator(MAGIC.T))
    half = pltpu.VMEM(HALF.shape, jnp.float32)
    return pl.pallas_call(
        scoped(back_kernel, accs_for(2, 2)),
        in_specs=[SMEM, ANY, ANY, ANY, ANY, ANY, HBM, HBM, HBM],
        out_specs=HBM,
        out_shape=jax.ShapeDtypeStruct(values.shape, jnp.float32),
        scratch_shapes=[*TABLES, ALL, ALL, TURNED, TURNED, PLANES, half, half, sems(3), sems(2, PIECES), sems(2, PIECES), sems(2, PIECES), sems(2)],
        compiler_params=params(52),
        cost_estimate=cost(57344, 26 * 2**20),
        name="back",
    )(core, *tables, own, other, values, kin0, kin1)


def kinetic(after, orbitals, group):
    z_table = np.concatenate([ONE_ROWS[MIXED], lane_operator(SIDES, MIXED)])
    x_table = np.concatenate([ONE_ROWS, lane_operator(SIDES)])
    specs, tables = constants(z_table, slow_operator(SIDES), x_table)
    return pl.pallas_call(
        scoped(functools.partial(kinetic_kernel, group), accs_for(4, 2)),
        in_specs=[SMEM, *specs, HBM],
        out_specs=HBM,
        out_shape=jax.ShapeDtypeStruct((GROUP, N, N * N), jnp.float32),
        scratch_shapes=[QUAD, TURNED, TURNED, sems(PIECES), sems(PIECES)],
        compiler_params=params(52),
        cost_estimate=cost(49152, 9 * 2**20),
        name=f"kinetic{group}",
    )(after, *tables, orbitals)


SWAP = [(0, 1), (1, 0)]


def on_device(orbitals, occupations, external):
    core = lax.axis_index("core").astype(jnp.int32).reshape(1)
    member = lax.axis_index("xl") * 4 + lax.axis_index("y")
    own_external = lax.dynamic_index_in_dim(external.reshape(4, 8, 4, 128).transpose(1, 2, 0, 3).reshape(8, 16, 128), member, 0, keepdims=False)
    values, keep, send = forward(core, occupations, orbitals)
    partial = keep + lax.ppermute(send, "core", SWAP)
    partial, after = lax.optimization_barrier((partial, core))
    shares = lax.all_to_all(partial, CHIPS, 0, 0, tiled=True)
    shares, kin0 = lax.optimization_barrier((shares, kinetic(after, orbitals, 0)))
    density = jnp.sum(shares, axis=0)
    potential = own_external - jnp.cbrt(3.0 / math.pi * density)
    copies, after = lax.optimization_barrier((jnp.broadcast_to(potential[None], (64, 16, 128)), core))
    own = lax.all_to_all(copies, CHIPS, 0, 0, tiled=True)
    own, kin1 = lax.optimization_barrier((own, kinetic(after, orbitals, 1)))
    other = lax.ppermute(own, "core", SWAP)
    return back(core, own, other, values, kin0, kin1)


def solution(mesh):
    fine = Mesh(mesh.devices.reshape(2, 4, 2, 2, 4), AXES)
    orb = ("xh", "z", "core")
    return jax.shard_map(
        on_device,
        mesh=fine,
        in_specs=(P(AXES, None, None), P(AXES), P(orb, None)),
        out_specs=P(AXES, None, None),
        check_vma=False,
    )
```

```python
import functools
import math

import jax
import jax.numpy as jnp
import ml_dtypes
import numpy as np
from jax import lax
from jax.experimental import pallas as pl
from jax.experimental.pallas import tpu as pltpu
from jax.sharding import Mesh, PartitionSpec as P

MAGIC_TAPS = [
    8.433424733352934e-07,
    -1.290557201342061e-05,
    8.76298447621056e-05,
    -0.00030158038132690465,
    0.001747237136729939,
    -0.009420470302010804,
    0.023738214637249424,
    0.0612625895831208,
    0.9940415697834003,
    -0.06048952891969835,
    -0.021030251609303816,
    0.013372634148547948,
    -0.0034412814449349387,
    0.0004944322768868992,
    -5.185986881173433e-05,
    2.7273449291197967e-06,
]
KINETIC_HALF = [
    -3.55369228991319,
    2.2191465938911166,
    -0.615614146557007,
    0.23717805821538057,
    -0.08226639997421234,
    0.022070291884822554,
    -0.004097656893426338,
    0.00045167920287502236,
    -2.3982285245075998e-05,
    2.0904234952920368e-06,
    -3.7230763047369276e-07,
    -1.0585705549674146e-08,
    -5.8138798302825403e-11,
    2.7080049362631943e-13,
    -6.9244749406392e-18,
]
KINETIC_TAPS = KINETIC_HALF[:0:-1] + KINETIC_HALF
SPACING = 0.45

N = 64
GROUP = 4
ROWS = GROUP * N
PAIRS = N // 2
BF16 = ml_dtypes.bfloat16
AXES = ("xh", "z", "core", "xl", "y")
CHIPS = ("xh", "xl", "y", "z")
PIECES = 2


def circulant(taps, offset):
    matrix = np.zeros((N, N), np.float32)
    for position, weight in enumerate(taps):
        for row in range(N):
            matrix[row, (row + position - offset) % N] += np.float32(weight)
    return matrix


def halves(matrix):
    high = matrix.astype(BF16)
    return high, (matrix - high.astype(np.float32)).astype(BF16)


MIXED = np.arange(128).reshape(2, 16, 4).transpose(1, 0, 2).reshape(128)


def lane_operator(matrix, order=slice(None)):
    return np.concatenate([np.concatenate([part, part], 1)[order] for part in halves(np.kron(np.eye(2, dtype=np.float32), matrix))])


def slow_operator(matrix):
    return np.concatenate(halves(np.kron(matrix, np.eye(4, dtype=np.float32))))


def window_operator(taps):
    band = np.zeros((16, 32), np.float32)
    for out in range(16):
        for position, weight in enumerate(taps):
            band[out, out + position] = np.float32(weight)
    return np.concatenate([np.concatenate([part, part], 1) for part in halves(np.kron(band, np.eye(4, dtype=np.float32)))])


MAGIC = circulant(MAGIC_TAPS, 8)
KINETIC = circulant(KINETIC_TAPS, 14) * np.float32(-0.5 / (SPACING * SPACING))
CENTRE = float(np.float32(3.0) * KINETIC[0, 0])
SIDES = KINETIC - np.diag(np.diag(KINETIC))
ONE = np.eye(N, dtype=np.float32)


def split(block):
    high = block.astype(jnp.bfloat16)
    return high, (block - high.astype(jnp.float32)).astype(jnp.bfloat16)


def both(block):
    return jnp.concatenate(split(block), axis=1)


def run(jobs):
    queues = []
    for unit, queue in enumerate(jobs):
        steps = []
        for index, (parts, accs, finish) in enumerate(queue):
            for at, part in enumerate(parts):
                steps.append((part, accs, finish if at == len(parts) - 1 else None))
        queues.append(steps)
    pending = [None] * len(queues)

    def push(unit, at):
        (operand, transpose, _), _, _ = queues[unit][at]
        pltpu.matmul_push_rhs(operand(), at % 2, unit, transpose=transpose)

    for unit in range(len(queues)):
        push(unit, 0)
    for at in range(len(queues[0])):
        for unit, queue in enumerate(queues):
            if at + 1 < len(queue):
                push(unit, at + 1)
            (_, _, products), accs, finish = queue[at]
            for which, (acc, left) in enumerate(products):
                pltpu.matmul_acc_lhs(accs[acc], left(), load_staged_rhs=at % 2 if which == 0 else None)
            if pending[unit] is not None:
                done, held = pending[unit]
                done(*[pltpu.matmul_pop(acc) for acc in held])
                pending[unit] = None
            if finish is not None:
                pending[unit] = (finish, accs)
    for done, held in pending:
        done(*[pltpu.matmul_pop(acc) for acc in held])


def part(ref, start, size):
    return lambda: ref[start : start + size]


def lanes_at(index, size):
    return pl.ds(pl.multiple_of(index * size, size), size)


def repeat(count, body):
    if count == 1:
        body(0)
    else:

        def step(index, _):
            body(index)
            return 0

        lax.fori_loop(0, count, step, 0)


def along_tiles(loops, operand, products, accs, target, before):
    count = PAIRS // loops // 2

    def body(index):
        before(index)

        def job(tile, unit, at):
            def finish(*outs):
                for ref, out in zip(target, outs):
                    ref[tile] = out.reshape(16, 8, ROWS)

            return ([(lambda: operand(tile), True, products)], accs[unit][at % 2], finish)

        run([[job((index * count + at) * 2 + unit, unit, at) for at in range(count)] for unit in range(2)])

    repeat(loops, body)


def along_slow(loops, source, target, op_ref, accs, add=None):
    count = 8 // loops

    def body(index):
        def job(block, unit, at):
            cache = []

            def high():
                cache.extend(split(source[:, block].reshape(256, ROWS)))
                return cache[0]

            def finish(out):
                out = out.reshape(PAIRS, 8, ROWS)
                target[:, block] = out if add is None else out + add[:, block]

            first = (high, False, [(0, part(op_ref, 0, 256)), (0, part(op_ref, 256, 256))])
            second = (lambda: cache[1], False, [(0, part(op_ref, 0, 256))])
            return ([first, second], [accs[unit][at % 2]], finish)

        run([[job((index * count + at) * 2 + unit, unit, at) for at in range(count)] for unit in range(2)])

    repeat(loops, body)


def natural(ref, index, pair):
    rows = []
    for tile in range(2):
        block = ref[index * 2 + tile, :, :, pair * 128 : pair * 128 + 128].reshape(8, 2, 8, 128)
        even, odd = block[:, 0], block[:, 1]
        upper = lax.broadcasted_iota(jnp.int32, even.shape, 1) < 4
        rows.append(jnp.where(upper, even, pltpu.roll(odd, 4, 1)).reshape(N, 128))
        rows.append(jnp.where(upper, pltpu.roll(even, 4, 1), odd).reshape(N, 128))
    return jnp.concatenate(rows, axis=0)


def along_windows(source, target, op_ref, accs):
    def job(block, unit, at):
        cache = []

        def window(start):
            def operand():
                if not cache:
                    cache.extend(split(source[:, block].reshape(256, ROWS)))
                low, high = start * 64 - 32, start * 64 + 96
                if low < 0:
                    rows = [(256 + low, 256), (0, high)]
                elif high > 256:
                    rows = [(low, 256), (0, high - 256)]
                else:
                    rows = [(low, high)]
                return jnp.concatenate([half[a:b] for half in cache for a, b in rows], axis=0)

            return (operand, False, [(start, part(op_ref, 0, 64)), (start, part(op_ref, 64, 64))])

        def finish(*outs):
            target[:, block] = jnp.concatenate(outs, axis=0).reshape(PAIRS, 8, ROWS)

        return ([window(start) for start in range(4)], accs[unit][at % 2 * 4 : at % 2 * 4 + 4], finish)

    run([[job(2 * at + unit, unit, at) for at in range(8)] for unit in range(2)])


def along_x(loops, steps_of, accs, finish_of, before, after):
    count = 16 // loops

    def body(index):
        before(index)

        def job(block, unit, at):
            return (steps_of(block, unit), [accs[unit][at % 2][0]], functools.partial(finish_of, block, unit))

        run([[job(index * count + at, unit, at) for at in range(count)] for unit in range(2)])
        after(index)

    repeat(loops, body)


def nothing(_):
    return None


def piece(group, index):
    return (pl.ds(group * GROUP, GROUP), slice(None), lanes_at(index, N * N // PIECES))


def places():
    for position in range(64):
        xh, xl, y, z = position // 32, position // 16 % 2, position // 4 % 4, position % 4
        for pair in range(2):
            yield position, (xh * 4 + z) * 8, (xl * 4 + y) * 4 + pair * 2, pair * 8


def exchange_halves(low, high):
    upper = lax.broadcasted_iota(jnp.int32, low.shape, 0) < 4
    return jnp.where(upper, low, pltpu.roll(high, 4, 0)), jnp.where(upper, pltpu.roll(low, 4, 0), high)


def forward_kernel(core_ref, occ_hbm, z_hbm, y_hbm, x_hbm, orb_hbm, val_hbm, keep_ref, send_ref, occ_ref, z_ref, y_ref, x_ref, orbs, first, second, total, ready, arrived, left, *accs):
    small, large = ((accs[0:1], accs[1:2]), (accs[2:3], accs[3:4])), (accs[4:12], accs[12:20])
    z_products = [(0, part(z_ref, 0, 128)), (0, part(z_ref, 128, 128))]
    x_products = [(0, part(x_ref, 0, 128)), (0, part(x_ref, 128, 128))]

    def fetch(group, index):
        return pltpu.make_async_copy(orb_hbm.at[piece(group, index)], orbs.at[piece(group, index)], arrived.at[group, index])

    def give(group, index):
        return pltpu.make_async_copy(orbs.at[piece(group, index)], val_hbm.at[piece(group, index)], left.at[group, index])

    tables = [
        pltpu.make_async_copy(source, target, ready.at[at])
        for at, (source, target) in enumerate(((z_hbm, z_ref), (y_hbm, y_ref), (x_hbm, x_ref), (occ_hbm, occ_ref)))
    ]
    tables[0].start()
    fetch(0, 0).start()
    fetch(0, 1).start()
    for table in tables[1:]:
        table.start()
    total[...] = jnp.zeros_like(total)
    tables[0].wait()

    def one_group(group, _):
        mine = orbs.at[pl.ds(group * GROUP, GROUP)]

        def operand(tile):
            if tile % (PAIRS // PIECES) == 0:
                fetch(group, tile // (PAIRS // PIECES)).wait()
            return both(mine[:, :, lanes_at(tile, 128)].reshape(ROWS, 128))

        along_tiles(1, operand, z_products, small, [first], nothing)

        @pl.when(group == 0)
        def _():
            for index in range(PIECES):
                fetch(1, index).start()
            for table in tables[1:]:
                table.wait()

        along_windows(first, second, y_ref, large)

        def finish(block, pair, out):
            lanes = lanes_at(block, 256)
            out = out.reshape(2, N, 256)
            mine[pair * 2 : pair * 2 + 2, :, lanes] = out
            weighted = [occ_ref[group * GROUP + pair * 2 + one] * (out[one] * out[one]) for one in range(2)]
            total[:, lanes] = total[:, lanes] + (weighted[0] + weighted[1])

        along_x(2, lambda block, pair: [(lambda: both(natural(second, block, pair)), True, x_products)], small, finish, nothing, lambda index: give(group, index).start())
        return 0

    lax.fori_loop(0, 2, one_group, 0)
    core = core_ref[0]
    for position, row, tile, at in places():
        low, high = [total[row : row + 8, one * 128 : one * 128 + 128] for one in (tile, tile + 1)]
        zero, one = exchange_halves(low, high)
        keep_ref[position, at : at + 8, :] = jnp.where(core == 0, zero, one)
        send_ref[position, at : at + 8, :] = jnp.where(core == 0, one, zero)
    for group in range(2):
        for index in range(PIECES):
            give(group, index).wait()


def back_kernel(core_ref, z_hbm, y_hbm, x_hbm, own_hbm, other_hbm, val_hbm, kin0_hbm, kin1_hbm, out_hbm, z_ref, y_ref, x_ref, vals, kins, first, second, total, own, other, ready, arrived, kin_arrived, left, halves_arrived, *accs):
    small, large = ((accs[0:1], accs[1:2]), (accs[2:3], accs[3:4])), (accs[4:12], accs[12:20])
    z_products = [(0, part(z_ref, 0, 128)), (0, part(z_ref, 128, 128))]
    x_products = [(0, part(x_ref, 0, 128)), (0, part(x_ref, 128, 128))]

    def fetch(group, index):
        return pltpu.make_async_copy(val_hbm.at[piece(group, index)], vals.at[piece(group, index)], arrived.at[group, index])

    def fetch_kin(which, index):
        source = (kin0_hbm, kin1_hbm)[which]
        return pltpu.make_async_copy(source.at[piece(0, index)], kins.at[piece(which, index)], kin_arrived.at[which, index])

    def give(group, index):
        return pltpu.make_async_copy(vals.at[piece(group, index)], out_hbm.at[piece(group, index)], left.at[group, index])

    pots = [pltpu.make_async_copy(source, target, halves_arrived.at[at]) for at, (source, target) in enumerate(((own_hbm, own), (other_hbm, other)))]
    tables = [
        pltpu.make_async_copy(source, target, ready.at[at]) for at, (source, target) in enumerate(((z_hbm, z_ref), (y_hbm, y_ref), (x_hbm, x_ref)))
    ]
    for copy in pots + tables[:1]:
        copy.start()
    fetch(0, 0).start()
    fetch(0, 1).start()
    for copy in tables[1:]:
        copy.start()
    for copy in pots:
        copy.wait()
    core = core_ref[0]
    for position, row, tile, at in places():
        mine, theirs = own[position, at : at + 8, :], other[position, at : at + 8, :]
        low, high = exchange_halves(jnp.where(core == 0, mine, theirs), jnp.where(core == 0, theirs, mine))
        total[row : row + 8, tile * 128 : tile * 128 + 128] = low
        total[row : row + 8, tile * 128 + 128 : tile * 128 + 256] = high
    tables[0].wait()

    def one_group(group, _):
        mine, kin = vals.at[pl.ds(group * GROUP, GROUP)], kins.at[pl.ds(group * GROUP, GROUP)]

        def operand(tile):
            if tile % (PAIRS // PIECES) == 0:
                fetch(group, tile // (PAIRS // PIECES)).wait()
            lanes = lanes_at(tile, 128)
            return both((mine[:, :, lanes] * total[:, lanes][None]).reshape(ROWS, 128))

        along_tiles(1, operand, z_products, small, [first], nothing)

        @pl.when(group == 0)
        def _():
            for index in range(PIECES):
                fetch_kin(0, index).start()
            for index in range(PIECES):
                fetch(1, index).start()
            for table in tables[1:]:
                table.wait()

        along_windows(first, second, y_ref, large)

        def before_x(index):
            for which in range(2):

                @pl.when(group == which)
                def _():
                    fetch_kin(which, index).wait()
                    if which == 0:
                        fetch_kin(1, index).start()

        def finish(block, pair, out):
            at = (slice(pair * 2, pair * 2 + 2), slice(None), lanes_at(block, 256))
            mine[at] = out.reshape(2, N, 256) + kin[at]

        along_x(2, lambda block, pair: [(lambda: both(natural(second, block, pair)), True, x_products)], small, finish, before_x, lambda index: give(group, index).start())
        return 0

    lax.fori_loop(0, 2, one_group, 0)
    for group in range(2):
        for index in range(PIECES):
            give(group, index).wait()


def kinetic_kernel(group, _, z_ref, y_ref, x_ref, orb_hbm, out_hbm, orbs, first, second, arrived, left, *accs):
    small, large = ((accs[0:2], accs[2:4]), (accs[4:6], accs[6:8])), (accs[8:10], accs[10:12])
    z_products = [(0, part(z_ref, 0, 128)), (1, part(z_ref, 128, 128)), (1, part(z_ref, 256, 128))]
    one_products = [(0, part(x_ref, 0, 128))]
    x_products = [(0, part(x_ref, 128, 128)), (0, part(x_ref, 256, 128))]
    def fetch(index):
        return pltpu.make_async_copy(orb_hbm.at[piece(group, index)], orbs.at[piece(0, index)], arrived.at[index])

    def give(index):
        return pltpu.make_async_copy(orbs.at[piece(0, index)], out_hbm.at[piece(0, index)], left.at[index])

    fetch(0).start()
    fetch(1).start()
    operand = lambda tile: both(orbs[:, :, lanes_at(tile, 128)].reshape(ROWS, 128))
    along_tiles(2, operand, z_products, small, [first, second], lambda index: fetch(index).wait())
    along_slow(1, first, second, y_ref, large, second)

    def steps(block, pair):
        return [
            (lambda: both(natural(second, block, pair)), True, one_products),
            (lambda: both(natural(first, block, pair)), True, x_products),
        ]

    def finish(block, pair, out):
        at = (slice(pair * 2, pair * 2 + 2), slice(None), lanes_at(block, 256))
        orbs[at] = out.reshape(2, N, 256) + CENTRE * orbs[at]

    along_x(2, steps, small, finish, nothing, lambda index: give(index).start())
    give(0).wait()
    give(1).wait()


SMEM = pl.BlockSpec(memory_space=pltpu.SMEM)
ANY = pl.BlockSpec(memory_space=pl.ANY)
HBM = pl.BlockSpec(memory_space=pltpu.HBM)
ALL = pltpu.VMEM((2 * GROUP, N, N * N), jnp.float32)
QUAD = pltpu.VMEM((GROUP, N, N * N), jnp.float32)
TURNED = pltpu.VMEM((PAIRS, 16, 8, ROWS), jnp.float32)
PLANES = pltpu.VMEM((N, N * N), jnp.float32)
HALF = jax.ShapeDtypeStruct((64, 16, 128), jnp.float32)
ONE_ROWS = lane_operator(ONE)[:128]


def scoped(kernel, accs):
    return lambda *refs: pl.run_scoped(functools.partial(kernel, *refs), *accs)


def accs_for(*counts):
    return [pltpu.ACC(unit)((rows, 256), jnp.float32) for rows, count in counts for unit in range(2) for _ in range(count)]


def whole(shape):
    return pl.BlockSpec(shape, lambda *_: (0,) * len(shape))


def cost(rows, bytes_accessed):
    return pl.CostEstimate(flops=rows * 2 * 256 * 256, bytes_accessed=bytes_accessed, transcendentals=0)


TABLES = [pltpu.VMEM((256, 256), jnp.bfloat16), pltpu.VMEM((128, 256), jnp.bfloat16), pltpu.VMEM((256, 256), jnp.bfloat16)]


def constants(*tables):
    return [whole(table.shape) for table in tables], [jnp.asarray(table) for table in tables]


def sems(*shape):
    return pltpu.SemaphoreType.DMA(shape)


def params(mib):
    return pltpu.CompilerParams(vmem_limit_bytes=mib * 2**20)


def forward(core, occupations, orbitals):
    _, tables = constants(lane_operator(MAGIC, MIXED), window_operator(MAGIC_TAPS), lane_operator(MAGIC))
    return pl.pallas_call(
        scoped(forward_kernel, accs_for((128, 2), (64, 8))),
        in_specs=[SMEM, ANY, ANY, ANY, ANY, HBM],
        out_specs=[HBM, whole(HALF.shape), whole(HALF.shape)],
        out_shape=[jax.ShapeDtypeStruct(orbitals.shape, jnp.float32), HALF, HALF],
        scratch_shapes=[pltpu.SMEM((2 * GROUP,), jnp.float32), *TABLES, ALL, TURNED, TURNED, PLANES, sems(4), sems(2, PIECES), sems(2, PIECES)],
        compiler_params=params(60),
        cost_estimate=cost(57344, 18 * 2**20),
        name="forward",
    )(core, occupations, *tables, orbitals)


def back(core, own, other, values, kin0, kin1):
    _, tables = constants(lane_operator(MAGIC.T, MIXED), window_operator([0.0] + MAGIC_TAPS[::-1]), lane_operator(MAGIC.T))
    half = pltpu.VMEM(HALF.shape, jnp.float32)
    return pl.pallas_call(
        scoped(back_kernel, accs_for((128, 2), (64, 8))),
        in_specs=[SMEM, ANY, ANY, ANY, ANY, ANY, HBM, HBM, HBM],
        out_specs=HBM,
        out_shape=jax.ShapeDtypeStruct(values.shape, jnp.float32),
        scratch_shapes=[*TABLES, ALL, ALL, TURNED, TURNED, PLANES, half, half, sems(3), sems(2, PIECES), sems(2, PIECES), sems(2, PIECES), sems(2)],
        compiler_params=params(52),
        cost_estimate=cost(57344, 26 * 2**20),
        name="back",
    )(core, *tables, own, other, values, kin0, kin1)


def kinetic(after, orbitals, group):
    z_table = np.concatenate([ONE_ROWS[MIXED], lane_operator(SIDES, MIXED)])
    x_table = np.concatenate([ONE_ROWS, lane_operator(SIDES)])
    specs, tables = constants(z_table, slow_operator(SIDES), x_table)
    return pl.pallas_call(
        scoped(functools.partial(kinetic_kernel, group), accs_for((128, 4), (256, 2))),
        in_specs=[SMEM, *specs, HBM],
        out_specs=HBM,
        out_shape=jax.ShapeDtypeStruct((GROUP, N, N * N), jnp.float32),
        scratch_shapes=[QUAD, TURNED, TURNED, sems(PIECES), sems(PIECES)],
        compiler_params=params(52),
        cost_estimate=cost(49152, 9 * 2**20),
        name=f"kinetic{group}",
    )(after, *tables, orbitals)


SWAP = [(0, 1), (1, 0)]


def on_device(orbitals, occupations, external):
    core = lax.axis_index("core").astype(jnp.int32).reshape(1)
    member = lax.axis_index("xl") * 4 + lax.axis_index("y")
    own_external = lax.dynamic_index_in_dim(external.reshape(4, 8, 4, 128).transpose(1, 2, 0, 3).reshape(8, 16, 128), member, 0, keepdims=False)
    values, keep, send = forward(core, occupations, orbitals)
    partial = keep + lax.ppermute(send, "core", SWAP)
    partial, after = lax.optimization_barrier((partial, core))
    shares = lax.all_to_all(partial, CHIPS, 0, 0, tiled=True)
    shares, kin0 = lax.optimization_barrier((shares, kinetic(after, orbitals, 0)))
    density = jnp.sum(shares, axis=0)
    potential = own_external - jnp.cbrt(3.0 / math.pi * density)
    copies, after = lax.optimization_barrier((jnp.broadcast_to(potential[None], (64, 16, 128)), core))
    own = lax.all_to_all(copies, CHIPS, 0, 0, tiled=True)
    own, kin1 = lax.optimization_barrier((own, kinetic(after, orbitals, 1)))
    other = lax.ppermute(own, "core", SWAP)
    return back(core, own, other, values, kin0, kin1)


def solution(mesh):
    fine = Mesh(mesh.devices.reshape(2, 4, 2, 2, 4), AXES)
    orb = ("xh", "z", "core")
    return jax.shard_map(
        on_device,
        mesh=fine,
        in_specs=(P(AXES, None, None), P(AXES), P(orb, None)),
        out_specs=P(AXES, None, None),
        check_vma=False,
    )
```

```python
import functools
import math

import jax
import jax.numpy as jnp
import ml_dtypes
import numpy as np
from jax import lax
from jax.experimental import pallas as pl
from jax.experimental.pallas import tpu as pltpu
from jax.sharding import Mesh, PartitionSpec as P

MAGIC_TAPS = [
    8.433424733352934e-07,
    -1.290557201342061e-05,
    8.76298447621056e-05,
    -0.00030158038132690465,
    0.001747237136729939,
    -0.009420470302010804,
    0.023738214637249424,
    0.0612625895831208,
    0.9940415697834003,
    -0.06048952891969835,
    -0.021030251609303816,
    0.013372634148547948,
    -0.0034412814449349387,
    0.0004944322768868992,
    -5.185986881173433e-05,
    2.7273449291197967e-06,
]
KINETIC_HALF = [
    -3.55369228991319,
    2.2191465938911166,
    -0.615614146557007,
    0.23717805821538057,
    -0.08226639997421234,
    0.022070291884822554,
    -0.004097656893426338,
    0.00045167920287502236,
    -2.3982285245075998e-05,
    2.0904234952920368e-06,
    -3.7230763047369276e-07,
    -1.0585705549674146e-08,
    -5.8138798302825403e-11,
    2.7080049362631943e-13,
    -6.9244749406392e-18,
]
KINETIC_TAPS = KINETIC_HALF[:0:-1] + KINETIC_HALF
SPACING = 0.45

N = 64
GROUP = 4
ROWS = GROUP * N
PAIRS = N // 2
BF16 = ml_dtypes.bfloat16
AXES = ("xh", "z", "core", "xl", "y")
CHIPS = ("xh", "xl", "y", "z")
PIECES = 2
GIVEN = 4


def circulant(taps, offset):
    matrix = np.zeros((N, N), np.float32)
    for position, weight in enumerate(taps):
        for row in range(N):
            matrix[row, (row + position - offset) % N] += np.float32(weight)
    return matrix


def halves(matrix):
    high = matrix.astype(BF16)
    return high, (matrix - high.astype(np.float32)).astype(BF16)


MIXED = np.arange(128).reshape(2, 16, 4).transpose(1, 0, 2).reshape(128)


def lane_operator(matrix, order=slice(None)):
    return np.concatenate([np.concatenate([part, part], 1)[order] for part in halves(np.kron(np.eye(2, dtype=np.float32), matrix))])


def slow_operator(matrix):
    return np.concatenate(halves(np.kron(matrix, np.eye(4, dtype=np.float32))))


def window_operator(taps):
    band = np.zeros((16, 32), np.float32)
    for out in range(16):
        for position, weight in enumerate(taps):
            band[out, out + position] = np.float32(weight)
    return np.concatenate([np.concatenate([part, part], 1) for part in halves(np.kron(band, np.eye(4, dtype=np.float32)))])


MAGIC = circulant(MAGIC_TAPS, 8)
KINETIC = circulant(KINETIC_TAPS, 14) * np.float32(-0.5 / (SPACING * SPACING))
CENTRE = float(np.float32(3.0) * KINETIC[0, 0])
SIDES = KINETIC - np.diag(np.diag(KINETIC))
ONE = np.eye(N, dtype=np.float32)


def split(block):
    high = block.astype(jnp.bfloat16)
    return high, (block - high.astype(jnp.float32)).astype(jnp.bfloat16)


def both(block):
    return jnp.concatenate(split(block), axis=1)


def run(jobs):
    queues = []
    for unit, queue in enumerate(jobs):
        steps = []
        for index, (parts, accs, finish) in enumerate(queue):
            for at, part in enumerate(parts):
                steps.append((part, accs, finish if at == len(parts) - 1 else None))
        queues.append(steps)
    pending = [None] * len(queues)

    def push(unit, at):
        (operand, transpose, _), _, _ = queues[unit][at]
        pltpu.matmul_push_rhs(operand(), at % 2, unit, transpose=transpose)

    for unit in range(len(queues)):
        push(unit, 0)
    for at in range(len(queues[0])):
        for unit, queue in enumerate(queues):
            if at + 1 < len(queue):
                push(unit, at + 1)
            (_, _, products), accs, finish = queue[at]
            for which, (acc, left) in enumerate(products):
                pltpu.matmul_acc_lhs(accs[acc], left(), load_staged_rhs=at % 2 if which == 0 else None)
            if pending[unit] is not None:
                done, held = pending[unit]
                done(*[pltpu.matmul_pop(acc) for acc in held])
                pending[unit] = None
            if finish is not None:
                pending[unit] = (finish, accs)
    for done, held in pending:
        done(*[pltpu.matmul_pop(acc) for acc in held])


def part(ref, start, size):
    return lambda: ref[start : start + size]


def lanes_at(index, size):
    return pl.ds(pl.multiple_of(index * size, size), size)


def repeat(count, body):
    if count == 1:
        body(0)
    else:

        def step(index, _):
            body(index)
            return 0

        lax.fori_loop(0, count, step, 0)


def along_tiles(loops, operand, products, accs, target, before):
    count = PAIRS // loops // 2

    def body(index):
        before(index)

        def job(tile, unit, at):
            def finish(*outs):
                for ref, out in zip(target, outs):
                    ref[tile] = out.reshape(16, 8, ROWS)

            return ([(lambda: operand(tile), True, products)], accs[unit][at % 2], finish)

        run([[job((index * count + at) * 2 + unit, unit, at) for at in range(count)] for unit in range(2)])

    repeat(loops, body)


def along_slow(loops, source, target, op_ref, accs, add=None):
    count = 8 // loops

    def body(index):
        def job(block, unit, at):
            cache = []

            def high():
                cache.extend(split(source[:, block].reshape(256, ROWS)))
                return cache[0]

            def finish(out):
                out = out.reshape(PAIRS, 8, ROWS)
                target[:, block] = out if add is None else out + add[:, block]

            first = (high, False, [(0, part(op_ref, 0, 256)), (0, part(op_ref, 256, 256))])
            second = (lambda: cache[1], False, [(0, part(op_ref, 0, 256))])
            return ([first, second], [accs[unit][at % 2]], finish)

        run([[job((index * count + at) * 2 + unit, unit, at) for at in range(count)] for unit in range(2)])

    repeat(loops, body)


def natural(ref, index, pair):
    rows = []
    for tile in range(2):
        block = ref[index * 2 + tile, :, :, pair * 128 : pair * 128 + 128].reshape(8, 2, 8, 128)
        even, odd = block[:, 0], block[:, 1]
        upper = lax.broadcasted_iota(jnp.int32, even.shape, 1) < 4
        rows.append(jnp.where(upper, even, pltpu.roll(odd, 4, 1)).reshape(N, 128))
        rows.append(jnp.where(upper, pltpu.roll(even, 4, 1), odd).reshape(N, 128))
    return jnp.concatenate(rows, axis=0)


def along_windows(source, target, op_ref, accs):
    def job(block, unit, at):
        cache = []

        def window(start):
            def operand():
                if not cache:
                    cache.extend(split(source[:, block].reshape(256, ROWS)))
                low, high = start * 64 - 32, start * 64 + 96
                if low < 0:
                    rows = [(256 + low, 256), (0, high)]
                elif high > 256:
                    rows = [(low, 256), (0, high - 256)]
                else:
                    rows = [(low, high)]
                return jnp.concatenate([half[a:b] for half in cache for a, b in rows], axis=0)

            return (operand, False, [(start, part(op_ref, 0, 64)), (start, part(op_ref, 64, 64))])

        def finish(*outs):
            target[:, block] = jnp.concatenate(outs, axis=0).reshape(PAIRS, 8, ROWS)

        return ([window(start) for start in range(4)], accs[unit][at % 2 * 4 : at % 2 * 4 + 4], finish)

    run([[job(2 * at + unit, unit, at) for at in range(8)] for unit in range(2)])


def along_x(loops, steps_of, accs, finish_of, before, after):
    count = 16 // loops

    def body(index):
        before(index)

        def job(block, unit, at):
            return (steps_of(block, unit), [accs[unit][at % 2][0]], functools.partial(finish_of, block, unit))

        run([[job(index * count + at, unit, at) for at in range(count)] for unit in range(2)])
        after(index)

    repeat(loops, body)


def nothing(_):
    return None


def piece(group, index, pieces=PIECES):
    return (pl.ds(group * GROUP, GROUP), slice(None), lanes_at(index, N * N // pieces))


def places():
    for position in range(64):
        xh, xl, y, z = position // 32, position // 16 % 2, position // 4 % 4, position % 4
        for pair in range(2):
            yield position, (xh * 4 + z) * 8, (xl * 4 + y) * 4 + pair * 2, pair * 8


def exchange_halves(low, high):
    upper = lax.broadcasted_iota(jnp.int32, low.shape, 0) < 4
    return jnp.where(upper, low, pltpu.roll(high, 4, 0)), jnp.where(upper, pltpu.roll(low, 4, 0), high)


def forward_kernel(core_ref, occ_hbm, z_hbm, y_hbm, x_hbm, orb_hbm, val_hbm, keep_ref, send_ref, occ_ref, z_ref, y_ref, x_ref, orbs, first, second, total, ready, arrived, left, *accs):
    small, large = ((accs[0:1], accs[1:2]), (accs[2:3], accs[3:4])), (accs[4:12], accs[12:20])
    z_products = [(0, part(z_ref, 0, 128)), (0, part(z_ref, 128, 128))]
    x_products = [(0, part(x_ref, 0, 128)), (0, part(x_ref, 128, 128))]

    def fetch(group, index):
        return pltpu.make_async_copy(orb_hbm.at[piece(group, index)], orbs.at[piece(group, index)], arrived.at[group, index])

    def give(group, index):
        return pltpu.make_async_copy(orbs.at[piece(group, index, GIVEN)], val_hbm.at[piece(group, index, GIVEN)], left.at[group, index])

    tables = [
        pltpu.make_async_copy(source, target, ready.at[at])
        for at, (source, target) in enumerate(((z_hbm, z_ref), (y_hbm, y_ref), (x_hbm, x_ref), (occ_hbm, occ_ref)))
    ]
    tables[0].start()
    fetch(0, 0).start()
    fetch(0, 1).start()
    for table in tables[1:]:
        table.start()
    total[...] = jnp.zeros_like(total)
    tables[0].wait()

    def one_group(group, _):
        mine = orbs.at[pl.ds(group * GROUP, GROUP)]

        def operand(tile):
            if tile % (PAIRS // PIECES) == 0:
                fetch(group, tile // (PAIRS // PIECES)).wait()
            return both(mine[:, :, lanes_at(tile, 128)].reshape(ROWS, 128))

        along_tiles(1, operand, z_products, small, [first], nothing)

        @pl.when(group == 0)
        def _():
            for index in range(PIECES):
                fetch(1, index).start()
            for table in tables[1:]:
                table.wait()

        along_windows(first, second, y_ref, large)

        def finish(block, pair, out):
            lanes = lanes_at(block, 256)
            out = out.reshape(2, N, 256)
            mine[pair * 2 : pair * 2 + 2, :, lanes] = out
            weighted = [occ_ref[group * GROUP + pair * 2 + one] * (out[one] * out[one]) for one in range(2)]
            total[:, lanes] = total[:, lanes] + (weighted[0] + weighted[1])
            if pair == 1 and block % (16 // GIVEN) == 16 // GIVEN - 1:
                give(group, block // (16 // GIVEN)).start()

        along_x(1, lambda block, pair: [(lambda: both(natural(second, block, pair)), True, x_products)], small, finish, nothing, nothing)
        return 0

    lax.fori_loop(0, 2, one_group, 0)
    core = core_ref[0]
    for position, row, tile, at in places():
        low, high = [total[row : row + 8, one * 128 : one * 128 + 128] for one in (tile, tile + 1)]
        zero, one = exchange_halves(low, high)
        keep_ref[position, at : at + 8, :] = jnp.where(core == 0, zero, one)
        send_ref[position, at : at + 8, :] = jnp.where(core == 0, one, zero)
    for group in range(2):
        for index in range(GIVEN):
            give(group, index).wait()


def back_kernel(core_ref, z_hbm, y_hbm, x_hbm, own_hbm, other_hbm, val_hbm, kin0_hbm, kin1_hbm, out_hbm, z_ref, y_ref, x_ref, vals, kins, first, second, total, own, other, ready, arrived, kin_arrived, left, halves_arrived, *accs):
    small, large = ((accs[0:1], accs[1:2]), (accs[2:3], accs[3:4])), (accs[4:12], accs[12:20])
    z_products = [(0, part(z_ref, 0, 128)), (0, part(z_ref, 128, 128))]
    x_products = [(0, part(x_ref, 0, 128)), (0, part(x_ref, 128, 128))]

    def fetch(group, index):
        return pltpu.make_async_copy(val_hbm.at[piece(group, index)], vals.at[piece(group, index)], arrived.at[group, index])

    def fetch_kin(which, index):
        source = (kin0_hbm, kin1_hbm)[which]
        return pltpu.make_async_copy(source.at[piece(0, index)], kins.at[piece(which, index)], kin_arrived.at[which, index])

    def give(group, index):
        return pltpu.make_async_copy(vals.at[piece(group, index, GIVEN)], out_hbm.at[piece(group, index, GIVEN)], left.at[group, index])

    pots = [pltpu.make_async_copy(source, target, halves_arrived.at[at]) for at, (source, target) in enumerate(((own_hbm, own), (other_hbm, other)))]
    tables = [
        pltpu.make_async_copy(source, target, ready.at[at]) for at, (source, target) in enumerate(((z_hbm, z_ref), (y_hbm, y_ref), (x_hbm, x_ref)))
    ]
    for copy in pots + tables[:1]:
        copy.start()
    fetch(0, 0).start()
    fetch(0, 1).start()
    for copy in tables[1:]:
        copy.start()
    for copy in pots:
        copy.wait()
    core = core_ref[0]
    for position, row, tile, at in places():
        mine, theirs = own[position, at : at + 8, :], other[position, at : at + 8, :]
        low, high = exchange_halves(jnp.where(core == 0, mine, theirs), jnp.where(core == 0, theirs, mine))
        total[row : row + 8, tile * 128 : tile * 128 + 128] = low
        total[row : row + 8, tile * 128 + 128 : tile * 128 + 256] = high
    tables[0].wait()

    def one_group(group, _):
        mine, kin = vals.at[pl.ds(group * GROUP, GROUP)], kins.at[pl.ds(group * GROUP, GROUP)]

        def operand(tile):
            if tile % (PAIRS // PIECES) == 0:
                fetch(group, tile // (PAIRS // PIECES)).wait()
            lanes = lanes_at(tile, 128)
            return both((mine[:, :, lanes] * total[:, lanes][None]).reshape(ROWS, 128))

        along_tiles(1, operand, z_products, small, [first], nothing)

        @pl.when(group == 0)
        def _():
            for index in range(PIECES):
                fetch_kin(0, index).start()
            for index in range(PIECES):
                fetch(1, index).start()
            for table in tables[1:]:
                table.wait()

        along_windows(first, second, y_ref, large)

        def before_x(_):
            for which in range(2):

                @pl.when(group == which)
                def _():
                    for index in range(PIECES):
                        fetch_kin(which, index).wait()
                        if which == 0:
                            fetch_kin(1, index).start()

        def finish(block, pair, out):
            at = (slice(pair * 2, pair * 2 + 2), slice(None), lanes_at(block, 256))
            mine[at] = out.reshape(2, N, 256) + kin[at]
            if pair == 1 and block % (16 // GIVEN) == 16 // GIVEN - 1:
                give(group, block // (16 // GIVEN)).start()

        along_x(1, lambda block, pair: [(lambda: both(natural(second, block, pair)), True, x_products)], small, finish, before_x, nothing)
        return 0

    lax.fori_loop(0, 2, one_group, 0)
    for group in range(2):
        for index in range(GIVEN):
            give(group, index).wait()


def kinetic_kernel(group, _, z_ref, y_ref, x_ref, orb_hbm, out_hbm, orbs, first, second, arrived, left, *accs):
    small, large = ((accs[0:2], accs[2:4]), (accs[4:6], accs[6:8])), (accs[8:10], accs[10:12])
    z_products = [(0, part(z_ref, 0, 128)), (1, part(z_ref, 128, 128)), (1, part(z_ref, 256, 128))]
    one_products = [(0, part(x_ref, 0, 128))]
    x_products = [(0, part(x_ref, 128, 128)), (0, part(x_ref, 256, 128))]
    def fetch(index):
        return pltpu.make_async_copy(orb_hbm.at[piece(group, index)], orbs.at[piece(0, index)], arrived.at[index])

    def give(index):
        return pltpu.make_async_copy(orbs.at[piece(0, index)], out_hbm.at[piece(0, index)], left.at[index])

    fetch(0).start()
    fetch(1).start()
    operand = lambda tile: both(orbs[:, :, lanes_at(tile, 128)].reshape(ROWS, 128))
    along_tiles(2, operand, z_products, small, [first, second], lambda index: fetch(index).wait())
    along_slow(1, first, second, y_ref, large, second)

    def steps(block, pair):
        return [
            (lambda: both(natural(second, block, pair)), True, one_products),
            (lambda: both(natural(first, block, pair)), True, x_products),
        ]

    def finish(block, pair, out):
        at = (slice(pair * 2, pair * 2 + 2), slice(None), lanes_at(block, 256))
        orbs[at] = out.reshape(2, N, 256) + CENTRE * orbs[at]

    along_x(2, steps, small, finish, nothing, lambda index: give(index).start())
    give(0).wait()
    give(1).wait()


SMEM = pl.BlockSpec(memory_space=pltpu.SMEM)
ANY = pl.BlockSpec(memory_space=pl.ANY)
HBM = pl.BlockSpec(memory_space=pltpu.HBM)
ALL = pltpu.VMEM((2 * GROUP, N, N * N), jnp.float32)
QUAD = pltpu.VMEM((GROUP, N, N * N), jnp.float32)
TURNED = pltpu.VMEM((PAIRS, 16, 8, ROWS), jnp.float32)
PLANES = pltpu.VMEM((N, N * N), jnp.float32)
HALF = jax.ShapeDtypeStruct((64, 16, 128), jnp.float32)
ONE_ROWS = lane_operator(ONE)[:128]


def scoped(kernel, accs):
    return lambda *refs: pl.run_scoped(functools.partial(kernel, *refs), *accs)


def accs_for(*counts):
    return [pltpu.ACC(unit)((rows, 256), jnp.float32) for rows, count in counts for unit in range(2) for _ in range(count)]


def whole(shape):
    return pl.BlockSpec(shape, lambda *_: (0,) * len(shape))


def cost(rows, bytes_accessed):
    return pl.CostEstimate(flops=rows * 2 * 256 * 256, bytes_accessed=bytes_accessed, transcendentals=0)


TABLES = [pltpu.VMEM((256, 256), jnp.bfloat16), pltpu.VMEM((128, 256), jnp.bfloat16), pltpu.VMEM((256, 256), jnp.bfloat16)]


def constants(*tables):
    return [whole(table.shape) for table in tables], [jnp.asarray(table) for table in tables]


def sems(*shape):
    return pltpu.SemaphoreType.DMA(shape)


def params(mib):
    return pltpu.CompilerParams(vmem_limit_bytes=mib * 2**20)


def forward(core, occupations, orbitals):
    _, tables = constants(lane_operator(MAGIC, MIXED), window_operator(MAGIC_TAPS), lane_operator(MAGIC))
    return pl.pallas_call(
        scoped(forward_kernel, accs_for((128, 2), (64, 8))),
        in_specs=[SMEM, ANY, ANY, ANY, ANY, HBM],
        out_specs=[HBM, whole(HALF.shape), whole(HALF.shape)],
        out_shape=[jax.ShapeDtypeStruct(orbitals.shape, jnp.float32), HALF, HALF],
        scratch_shapes=[pltpu.SMEM((2 * GROUP,), jnp.float32), *TABLES, ALL, TURNED, TURNED, PLANES, sems(4), sems(2, PIECES), sems(2, GIVEN)],
        compiler_params=params(60),
        cost_estimate=cost(57344, 18 * 2**20),
        name="forward",
    )(core, occupations, *tables, orbitals)


def back(core, own, other, values, kin0, kin1):
    _, tables = constants(lane_operator(MAGIC.T, MIXED), window_operator([0.0] + MAGIC_TAPS[::-1]), lane_operator(MAGIC.T))
    half = pltpu.VMEM(HALF.shape, jnp.float32)
    return pl.pallas_call(
        scoped(back_kernel, accs_for((128, 2), (64, 8))),
        in_specs=[SMEM, ANY, ANY, ANY, ANY, ANY, HBM, HBM, HBM],
        out_specs=HBM,
        out_shape=jax.ShapeDtypeStruct(values.shape, jnp.float32),
        scratch_shapes=[*TABLES, ALL, ALL, TURNED, TURNED, PLANES, half, half, sems(3), sems(2, PIECES), sems(2, PIECES), sems(2, GIVEN), sems(2)],
        compiler_params=params(52),
        cost_estimate=cost(57344, 26 * 2**20),
        name="back",
    )(core, *tables, own, other, values, kin0, kin1)


def kinetic(after, orbitals, group):
    z_table = np.concatenate([ONE_ROWS[MIXED], lane_operator(SIDES, MIXED)])
    x_table = np.concatenate([ONE_ROWS, lane_operator(SIDES)])
    specs, tables = constants(z_table, slow_operator(SIDES), x_table)
    return pl.pallas_call(
        scoped(functools.partial(kinetic_kernel, group), accs_for((128, 4), (256, 2))),
        in_specs=[SMEM, *specs, HBM],
        out_specs=HBM,
        out_shape=jax.ShapeDtypeStruct((GROUP, N, N * N), jnp.float32),
        scratch_shapes=[QUAD, TURNED, TURNED, sems(PIECES), sems(PIECES)],
        compiler_params=params(52),
        cost_estimate=cost(49152, 9 * 2**20),
        name=f"kinetic{group}",
    )(after, *tables, orbitals)


SWAP = [(0, 1), (1, 0)]


def on_device(orbitals, occupations, external):
    core = lax.axis_index("core").astype(jnp.int32).reshape(1)
    member = lax.axis_index("xl") * 4 + lax.axis_index("y")
    own_external = lax.dynamic_index_in_dim(external.reshape(4, 8, 4, 128).transpose(1, 2, 0, 3).reshape(8, 16, 128), member, 0, keepdims=False)
    values, keep, send = forward(core, occupations, orbitals)
    partial = keep + lax.ppermute(send, "core", SWAP)
    partial, after = lax.optimization_barrier((partial, core))
    shares = lax.all_to_all(partial, CHIPS, 0, 0, tiled=True)
    shares, kin0 = lax.optimization_barrier((shares, kinetic(after, orbitals, 0)))
    density = jnp.sum(shares, axis=0)
    potential = own_external - jnp.cbrt(3.0 / math.pi * density)
    copies, after = lax.optimization_barrier((jnp.broadcast_to(potential[None], (64, 16, 128)), core))
    own = lax.all_to_all(copies, CHIPS, 0, 0, tiled=True)
    own, kin1 = lax.optimization_barrier((own, kinetic(after, orbitals, 1)))
    other = lax.ppermute(own, "core", SWAP)
    return back(core, own, other, values, kin0, kin1)


def solution(mesh):
    fine = Mesh(mesh.devices.reshape(2, 4, 2, 2, 4), AXES)
    orb = ("xh", "z", "core")
    return jax.shard_map(
        on_device,
        mesh=fine,
        in_specs=(P(AXES, None, None), P(AXES), P(orb, None)),
        out_specs=P(AXES, None, None),
        check_vma=False,
    )
```
